128 devices in a mesh: depth: 2 (over core), tile: 64 (over x, y, z).
Axes of the slice: x: 4, y: 4, z: 4, core: 2. Of those that a mesh axis runs over, the one named last changes fastest.
Arguments:
- specimen_layers: float32 [8, 2, 8192, 512], P('depth', None, 'tile'), may hold values from -1.2 to 2
- illumination_field: float32 [2, 128, 128], replicated, may hold values from -6 to 6
- propagator_spectral_angle: float32 [128, 128], replicated, may hold values from -3.140625 to 3.140625
- recorded_intensities: float32 [512, 128, 128], P('tile'), may hold values from 0 to 4
- patch_upper_edges: int32 [512], P('tile'), may hold values from 0 to 127
- patch_left_edges: int32 [512], P('tile'), may hold values from 0 to 384
- occupied_places_per_band: int32 [64], P('tile'), may hold values from 1 to 8, 256 in all
Outputs:
- obj_grad: float32 [8, 2, 8192, 512], P('depth', None, 'tile')
The draws below stay inside these ranges and needn't reach their ends.
Inputs may be any that keep to these rules, and one draw needn't show every extreme that they name: Slots q % 8 < occupied_places_per_band[t] of strip t are live, the others are ignored; some strip has all 8 slots live.
All inputs are finite; a program needn't handle non-finite values. No bound on the sum of `occupied_places_per_band` on one device may be relied on, other than what follows from the above.
Results may differ from the reference program's by a relative error of at most 0.0003.
Values sent between devices are 32-bit elements; how exact they have to be, the bound alone decides.
No kernel may reach another device: no remote copies, remote signals or barrier semaphores. Data moves between devices by JAX's collectives and lax.ppermute only.
A program may use at most 128 MiB of HBM per device.

```python
import math
import jax
import jax.numpy as jnp
import numpy as np
from jax import lax

PATCH_EDGE_SIZE = 128
ROWS_DEV = 128
COLS = 512
POS_DEV = 8
SLICES = 8
NROWS = 8192
PLACE_CAPACITY = 512
N_TILE = 64


def draw_specimen_layers(key, part):
    noise_key = jax.random.fold_in(key, 17)
    shape_full = (SLICES, 2, NROWS, COLS)
    noise_field = jnp.clip(0.4 * jax.random.normal(noise_key, shape_full, jnp.float32), -1.2, 1.2)
    offset_table = jnp.array([0.8, 0.0], jnp.float32).reshape(1, 2, 1, 1)
    return offset_table + noise_field


def with_ends(entries, own_key, least, largest):
    extent = entries.shape
    spot = [jax.random.randint(jax.random.fold_in(own_key, axis), (), 0, extent[axis]) for axis in range(len(extent))]
    entries = entries.at[tuple(spot)].set(least)
    longest = extent.index(max(extent))
    spot[longest] = (spot[longest] + 1) % extent[longest]
    return entries.at[tuple(spot)].set(largest)


def shard_levels(own_key, dims, cuts, smallest, high):
    def one(dim, blocks):
        draws = jax.random.uniform(jax.random.fold_in(jax.random.fold_in(own_key, 6), dim), (blocks,), jnp.float32, smallest / len(cuts), high / len(cuts))
        return jnp.repeat(jnp.exp(draws), dims[dim] // blocks).reshape((-1,) + (1,) * (len(dims) - dim - 1))

    gain = one(*cuts[0])
    for cut in cuts[1:]:
        gain = gain * one(*cut)
    return gain


def length_profile(amount, total, reach, slope):
    weights = [(1 << 20) // math.isqrt(standing ** slope) + 1 for standing in range(2, amount + 1)]
    surplus, holding = total - reach - (amount - 1), [1] * (amount - 1)
    while surplus > 0:
        candidates = [i for i in range(amount - 1) if holding[i] < reach]
        whole, remaining = sum([weights[i] for i in candidates]), surplus
        for i in candidates:
            extra = min(reach - holding[i], max(1, remaining * weights[i] // whole), surplus)
            holding[i] = holding[i] + extra
            surplus = surplus - extra
    return np.array([reach] + holding)


def uneven(key, count, total, bound, skew):
    if count == 2:
        one = jax.random.randint(key, (), max(1, total - bound), min(bound, total - 1) + 1)
        return jnp.stack([one, total - one])
    lengths = jnp.asarray(length_profile(count, total, bound, skew), jnp.int32)
    twos = (count - 1) // 2
    giver, sink = lengths[1:1 + 2 * twos:2], lengths[2:2 + 2 * twos:2]
    slack = jnp.minimum(giver - 1, bound - sink)
    passed = jax.random.randint(jax.random.fold_in(key, 1), (twos,), 0, 1 << 20) % (slack + 1)
    lengths = lengths.at[1:1 + 2 * twos:2].set(giver - passed).at[2:2 + 2 * twos:2].set(sink + passed)
    return lengths[jax.random.permutation(jax.random.fold_in(key, 2), count)]


def normal_values(own_key, shape, deviation, reach, kind=jnp.bfloat16):
    return jnp.clip(deviation * jax.random.normal(own_key, shape, jnp.float32), -reach, reach).astype(kind)


def setup_inputs(seed: int = 0) -> dict:
    arg_keys = jax.random.split(jax.random.key(seed), 8)
    return {
        "specimen_layers": draw_specimen_layers(jax.random.fold_in(arg_keys[7], 71), 0),
        "illumination_field": normal_values(arg_keys[1], (2, PATCH_EDGE_SIZE, PATCH_EDGE_SIZE), 1.0, 6.0, jnp.float32),
        "propagator_spectral_angle": jnp.clip(jax.random.uniform(arg_keys[2], (PATCH_EDGE_SIZE, PATCH_EDGE_SIZE), jnp.float32, -3.140625, 3.140625), -3.140625, 3.140625),
        "recorded_intensities": jnp.clip(4.0 * jax.random.uniform(arg_keys[3], (PLACE_CAPACITY, PATCH_EDGE_SIZE, PATCH_EDGE_SIZE), jnp.float32) ** shard_levels(arg_keys[3], (PLACE_CAPACITY, PATCH_EDGE_SIZE, PATCH_EDGE_SIZE), ((0, 64),), -0.2, 0.2), 0.0, 4.0),
        "patch_upper_edges": with_ends(jax.random.randint(arg_keys[4], (PLACE_CAPACITY,), 0, ROWS_DEV), jax.random.fold_in(arg_keys[4], 1), 0, ROWS_DEV - 1).astype(jnp.int32),
        "patch_left_edges": with_ends(jax.random.randint(arg_keys[5], (PLACE_CAPACITY,), 0, COLS - PATCH_EDGE_SIZE + 1), jax.random.fold_in(arg_keys[5], 1), 0, COLS - PATCH_EDGE_SIZE).astype(jnp.int32),
        "occupied_places_per_band": uneven(arg_keys[6], N_TILE, N_TILE * POS_DEV // 2, POS_DEV, 2).astype(jnp.int32),
    }


def propagate(wave_field, phase_field):
    spectrum = jnp.fft.fft2(wave_field, norm="ortho")
    return jnp.fft.ifft2(phase_field * spectrum, norm="ortho")


def reference(specimen_layers, illumination_field, propagator_spectral_angle, recorded_intensities, patch_upper_edges, patch_left_edges, occupied_places_per_band):
    window = illumination_field.shape[-1]
    slot_total = patch_upper_edges.shape[0]
    layers = specimen_layers.shape[0]
    total_rows = specimen_layers.shape[2]
    padded = jnp.pad(specimen_layers, ((0, 0), (0, 0), (0, window), (0, 0)))
    field = lax.complex(padded[:, 0], padded[:, 1])
    kernel = lax.complex(jnp.cos(propagator_spectral_angle), jnp.sin(propagator_spectral_angle))
    start_wave = lax.complex(illumination_field[0], illumination_field[1])
    slot_ids = jnp.arange(slot_total, dtype=jnp.int32)
    owner = slot_ids // POS_DEV
    occupied_place_flags = ((slot_ids % POS_DEV) < occupied_places_per_band[owner]).astype(jnp.float32)
    absolute_line_number = (patch_upper_edges + owner * ROWS_DEV).astype(jnp.int32)

    def lone_placement_term(layer_derivative, inputs):
        row_start, col_start, measured, weight = inputs
        anchor = jnp.zeros((), jnp.int32)
        patch = lax.dynamic_slice(field, (anchor, row_start, col_start), (layers, window, window))
        history = []
        wave_field = start_wave
        for layer_index in range(layers):
            history.append(wave_field)
            wave_field = wave_field * patch[layer_index]
            if layer_index < layers - 1:
                wave_field = propagate(wave_field, kernel)
        far_field = jnp.fft.fft2(wave_field, norm="ortho")
        excess = weight * (jnp.real(far_field) ** 2 + jnp.imag(far_field) ** 2 - measured)
        error = jnp.fft.ifft2(excess * far_field, norm="ortho")
        pieces = [None] * layers
        carried = error
        for layer_index in reversed(range(layers)):
            if layer_index < layers - 1:
                error = propagate(carried, jnp.conj(kernel))
            pieces[layer_index] = jnp.conj(history[layer_index]) * error
            carried = jnp.conj(patch[layer_index]) * error
        update = jnp.stack(pieces)
        current = lax.dynamic_slice(layer_derivative, (anchor, row_start, col_start), (layers, window, window))
        layer_derivative = lax.dynamic_update_slice(layer_derivative, current + update, (anchor, row_start, col_start))
        return layer_derivative, None

    layer_derivative = jnp.zeros(field.shape, field.dtype)
    layer_derivative, unused_output = lax.scan(lone_placement_term, layer_derivative, (absolute_line_number, patch_left_edges.astype(jnp.int32), recorded_intensities, occupied_place_flags))
    layer_derivative = layer_derivative[:, :total_rows]
    return jnp.stack([jnp.real(layer_derivative), jnp.imag(layer_derivative)], axis=1).astype(jnp.float32)
```

```python
import functools
import math

import jax
import jax.numpy as jnp
import numpy as np
from jax import lax
from jax.experimental import pallas as pl
from jax.experimental.pallas import tpu as pltpu
from jax.sharding import PartitionSpec as P


W = 128
S = 8
HALF = 64
TALL = 320
BLOCKS = 4

def tables():
    k = np.arange(W)
    a = (k[:, None] * k[None, :] % W) * (2 * math.pi / W)
    cr = np.cos(a) / math.sqrt(W)
    ci = -np.sin(a) / math.sqrt(W)
    right = np.block([[cr, ci], [-ci, cr]]).astype(np.float32)
    both = np.stack([right, right.T])
    hi = both.astype(jnp.bfloat16)
    lo = (both - hi.astype(np.float32)).astype(jnp.bfloat16)
    return np.stack([hi, lo], 1)

def split(x):
    hi = x.astype(jnp.bfloat16)
    lo = (x - hi.astype(jnp.float32)).astype(jnp.bfloat16)
    return hi, lo

def dot(a, b):
    return jnp.dot(a, b, preferred_element_type=jnp.float32)

def right_stage(rows_hi, rows_lo, tab, inv):
    th, tl = tab[inv, 0], tab[inv, 1]
    return dot(rows_hi, th) + dot(rows_lo, th) + dot(rows_hi, tl)

def left_stage(b_hi, b_lo, tab, inv):
    th, tl = tab[1 - inv, 0], tab[1 - inv, 1]
    return dot(th, b_hi) + dot(tl, b_hi) + dot(th, b_lo)

def to_pairs(y, pairs):
    out = []
    for p in range(pairs):
        a = y[p * 256:p * 256 + 128]
        b = y[p * 256 + 128:p * 256 + 256]
        out.append(jnp.concatenate([
            jnp.concatenate([a[:, :128], b[:, :128]], 1),
            jnp.concatenate([a[:, 128:], b[:, 128:]], 1)], 0))
    return out

def from_pairs(bs):
    rows = []
    for z in bs:
        rows.append(jnp.concatenate([z[:128, :128], z[128:, :128]], 1))
        rows.append(jnp.concatenate([z[:128, 128:], z[128:, 128:]], 1))
    return jnp.concatenate(rows, 0)

def sandwich(x, tab, mid):
    pairs = x.shape[0] // 256
    y = right_stage(*split(x), tab, 0)
    bs = to_pairs(y, pairs)
    zs = []
    for p, b in enumerate(bs):
        z = left_stage(*split(b), tab, 0)
        zr, zi = mid(p, z[:128], z[128:])
        z = jnp.concatenate([zr, zi], 0)
        zs.append(left_stage(*split(z), tab, 1))
    return right_stage(*split(from_pairs(zs)), tab, 1)

def cut(obj, s, comp, R, C):
    blk = jnp.minimum(C // W, 2)
    sh = C - blk * W
    turn = (W - sh) % W
    left = pltpu.roll(obj[s, comp, blk, pl.ds(R, W), :], turn, 1)
    right = pltpu.roll(obj[s, comp, blk + 1, pl.ds(R, W), :], turn, 1)
    lane = lax.broadcasted_iota(jnp.int32, (W, W), 1)
    return jnp.where(lane < W - sh, left, right)

def put(acc, s, comp, R, C, g):
    blk = jnp.minimum(C // W, 2)
    sh = C - blk * W
    turned = pltpu.roll(g, sh % W, 1)
    lane = lax.broadcasted_iota(jnp.int32, (W, W), 1)
    la = (s, comp, blk, pl.ds(R, W), slice(None))
    lb = (s, comp, blk + 1, pl.ds(R, W), slice(None))
    acc[la] = acc[la] + jnp.where(lane >= sh, turned, 0.0)
    acc[lb] = acc[lb] + jnp.where(lane < sh, turned, 0.0)

def group(G, first, n, offs, cols, srcs, obj, probe, H, inten, tab, acc, hist):
    pairs = G // 2
    idx = [jnp.minimum(first + j, n - 1) for j in range(G)]
    Rs = [offs[i] for i in idx]
    Cs = [cols[i] for i in idx]
    Is = [srcs[i] for i in idx]
    prow = jnp.concatenate([probe[0], probe[1]], 1)
    hist[0, :G * W, :] = jnp.concatenate([prow] * G, 0)

    def phi(s):
        rows = []
        for j in range(G):
            pr = hist[s, j * W:(j + 1) * W, :W]
            pi = hist[s, j * W:(j + 1) * W, W:]
            qr = cut(obj, s, 0, Rs[j], Cs[j])
            qi = cut(obj, s, 1, Rs[j], Cs[j])
            rows.append(jnp.concatenate([pr * qr - pi * qi, pr * qi + pi * qr], 1))
        return jnp.concatenate(rows, 0)

    def times_h(sign):
        def mid(p, zr, zi):
            hr = jnp.concatenate([H[0], H[0]], 1)
            hi = jnp.concatenate([H[1], H[1]], 1) * sign
            return zr * hr - zi * hi, zr * hi + zi * hr
        return mid

    def fwd(s, _):
        hist[s + 1, :G * W, :] = sandwich(phi(s), tab, times_h(1.0))
        return 0

    lax.fori_loop(0, S - 1, fwd, 0)

    def chi(p, zr, zi):
        meas = jnp.concatenate([inten[Is[2 * p]], inten[Is[2 * p + 1]]], 1)
        ex = zr * zr + zi * zi - meas
        return zr * ex, zi * ex

    hist[S, :G * W, :] = sandwich(phi(S - 1), tab, chi)

    def emit(s):
        rows = []
        for j in range(G):
            er = hist[S, j * W:(j + 1) * W, :W]
            ei = hist[S, j * W:(j + 1) * W, W:]
            pr = hist[s, j * W:(j + 1) * W, :W]
            pi = hist[s, j * W:(j + 1) * W, W:]
            qr = cut(obj, s, 0, Rs[j], Cs[j])
            qi = cut(obj, s, 1, Rs[j], Cs[j])
            @pl.when(first + j < n)
            def _():
                put(acc, s, 0, Rs[j], Cs[j], pr * er + pi * ei)
                put(acc, s, 1, Rs[j], Cs[j], pr * ei - pi * er)
            rows.append(jnp.concatenate([qr * er + qi * ei, qr * ei - qi * er], 1))
        return jnp.concatenate(rows, 0)

    def bwd(k, _):
        s = S - 1 - k
        hist[S, :G * W, :] = sandwich(emit(s), tab, times_h(-1.0))
        return 0

    lax.fori_loop(0, S - 1, bwd, 0)
    for j in range(G):
        er = hist[S, j * W:(j + 1) * W, :W]
        ei = hist[S, j * W:(j + 1) * W, W:]
        @pl.when(first + j < n)
        def _():
            pr, pi = probe[0], probe[1]
            put(acc, 0, 0, Rs[j], Cs[j], pr * er + pi * ei)
            put(acc, 0, 1, Rs[j], Cs[j], pr * ei - pi * er)


def plan(place, mine, prev, offs, cols, srcs):
    d, t, last = place[0], place[1], place[2]
    stays = [(q < mine[16]) & ((mine[q] <= HALF) | (t == last)) for q in range(8)]
    comes = [(q < prev[16]) & (prev[q] > HALF) for q in range(8)]
    one = [jnp.where(c, 1, 0) for c in stays]
    two = [jnp.where(c, 1, 0) for c in comes]
    own = sum(one)
    x0 = sum(two[0::2])
    x1 = sum(two[1::2])
    a0 = jnp.clip((own + x0 + x1 + 1) // 2 - x0, 0, own)
    low = jnp.where(d == 0, 0, a0)
    high = jnp.where(d == 0, a0, own)
    n = jnp.int32(0)
    for q in range(8):
        take = comes[q] & (d == q % 2)

        @pl.when(take)
        def _(q=q, n=n):
            offs[n] = prev[q] - HALF
            cols[n] = prev[8 + q]
            srcs[n] = 8 + q // 2

        n = n + jnp.where(take, 1, 0)
    rank = jnp.int32(0)
    for q in range(8):
        take = stays[q] & (rank >= low) & (rank < high)

        @pl.when(take)
        def _(q=q, n=n):
            offs[n] = mine[q] + HALF
            cols[n] = mine[8 + q]
            srcs[n] = q

        n = n + jnp.where(take, 1, 0)
        rank = rank + one[q]
    return n


SPANS = ((0, 64), (64, 128), (192, 64))


def main_kernel(place, mine, prev, *refs):
    ins = refs[:6]
    own_int, got_int, probe, H, tab = refs[6:11]
    outs = refs[11:17]
    obj, acc, hist, inten, offs, cols, srcs, sem = refs[17:]
    d = place[0]
    copies = []

    def start(a, b):
        c = pltpu.make_async_copy(a, b, sem.at[len(copies)])
        c.start()
        copies.append(c)

    for who in range(2):
        base = jnp.where(who == 0, d, 1 - d) * 4
        for k, (row, rows) in enumerate(SPANS):
            for cb in range(BLOCKS):
                start(
                    ins[who * 3 + k].at[:, :, :, pl.ds(cb * W, W)],
                    obj.at[pl.ds(base, 4), :, cb, pl.ds(row, rows), :],
                )
    start(own_int, inten.at[pl.ds(0, 8)])
    start(got_int, inten.at[pl.ds(8, 4)])
    n = plan(place, mine, prev, offs, cols, srcs)
    acc[...] = jnp.zeros_like(acc)
    obj[:, :, :, 256:, :] = jnp.zeros((S, 2, BLOCKS, TALL - 256, W), jnp.float32)
    for c in copies:
        c.wait()

    def work(first):
        left = n - first
        size = jnp.where(left > 4, 6, jnp.where(left > 2, 4, 2))
        for G in (2, 4, 6):

            @pl.when(size == G)
            def _(G=G):
                group(G, first, n, offs, cols, srcs, obj, probe, H, inten, tab, acc, hist)

        return first + size

    lax.while_loop(lambda first: first < n, work, jnp.int32(0))
    copies.clear()
    for who in range(2):
        base = jnp.where(who == 0, d, 1 - d) * 4
        for k, (row, rows) in enumerate(SPANS):
            for cb in range(BLOCKS):
                start(
                    acc.at[pl.ds(base, 4), :, cb, pl.ds(row, rows), :],
                    outs[who * 3 + k].at[:, :, :, pl.ds(cb * W, W)],
                )
    for c in copies:
        c.wait()


def shifted(value, axis, by):
    count = lax.axis_size(axis)
    pairs = [(i, i + by) for i in range(count) if 0 <= i + by < count]
    return lax.ppermute(value, axis, pairs)


def partner(value):
    return lax.ppermute(value, "depth", [(0, 1), (1, 0)])


def local(
    specimen_layers,
    illumination_field,
    propagator_spectral_angle,
    recorded_intensities,
    patch_upper_edges,
    patch_left_edges,
    occupied_places_per_band,
):
    depth = lax.axis_index("depth")
    tile = lax.axis_index("tile")
    place = jnp.stack([depth, tile, jnp.int32(lax.axis_size("tile") - 1)]).astype(jnp.int32)
    mine = jnp.concatenate([patch_upper_edges, patch_left_edges, occupied_places_per_band])
    prev = shifted(mine, "tile", 1)
    rim_next = shifted(specimen_layers[:, :, :HALF], "tile", -1)
    rim_prev = shifted(specimen_layers[:, :, HALF:], "tile", 1)
    sent_int = lax.dynamic_index_in_dim(
        recorded_intensities.reshape(4, 2, W, W), depth, 1, keepdims=False
    )
    got_int = shifted(sent_int, "tile", 1)
    other = partner(specimen_layers)
    other_next = partner(rim_next)
    other_prev = partner(rim_prev)
    H = jnp.stack([jnp.cos(propagator_spectral_angle), jnp.sin(propagator_spectral_angle)])
    hbm = pl.BlockSpec(memory_space=pl.ANY)
    vm = pl.BlockSpec(memory_space=pltpu.VMEM)
    sm = pl.BlockSpec(memory_space=pltpu.SMEM)
    parts = [
        jax.ShapeDtypeStruct((4, 2, rows, specimen_layers.shape[3]), jnp.float32)
        for row, rows in SPANS
    ]
    outs = pl.pallas_call(
        main_kernel,
        out_shape=parts + parts,
        in_specs=[sm] * 3 + [hbm] * 8 + [vm] * 3,
        out_specs=[hbm] * 6,
        scratch_shapes=[
            pltpu.VMEM((S, 2, BLOCKS, TALL, W), jnp.float32),
            pltpu.VMEM((S, 2, BLOCKS, TALL, W), jnp.float32),
            pltpu.VMEM((S + 1, 6 * W, 2 * W), jnp.float32),
            pltpu.VMEM((12, W, W), jnp.float32),
            pltpu.SMEM((8,), jnp.int32),
            pltpu.SMEM((8,), jnp.int32),
            pltpu.SMEM((8,), jnp.int32),
            pltpu.SemaphoreType.DMA((32,)),
        ],
        compiler_params=pltpu.CompilerParams(vmem_limit_bytes=60 * 1024 * 1024),
        name="slots",
    )(
        place, mine, prev,
        rim_prev, specimen_layers, rim_next,
        other_prev, other, other_next,
        recorded_intensities, got_int, illumination_field, H, jnp.asarray(tables()),
    )
    up = outs[0] + partner(outs[3])
    down = outs[2] + partner(outs[5])
    from_next = shifted(up, "tile", -1)
    from_prev = shifted(down, "tile", 1)
    own = outs[1] + partner(outs[4])
    return own + jnp.concatenate([from_prev, from_next], axis=2)


def solution(mesh):
    placed = (
        P("depth", None, "tile", None),
        P(),
        P(),
        P("tile", None, None),
        P("tile"),
        P("tile"),
        P("tile"),
    )
    return jax.shard_map(
        local, mesh=mesh, in_specs=placed, out_specs=P("depth", None, "tile", None), check_vma=False
    )
```

```python
import math

import jax
import jax.numpy as jnp
import numpy as np
from jax import lax
from jax.experimental import pallas as pl
from jax.experimental.pallas import tpu as pltpu
from jax.sharding import PartitionSpec as P


W = 128
HALF = 64
TALL = 320
BLOCKS = 4
GROUP = 4
SIZES = (5, 6)
ROOM = 10
SPANS = ((0, 64), (64, 128), (192, 64))


def tables():
    k = np.arange(W)
    a = (k[:, None] * k[None, :] % W) * (2 * math.pi / W)
    cr = np.cos(a) / math.sqrt(W)
    ci = -np.sin(a) / math.sqrt(W)
    right = np.block([[cr, ci], [-ci, cr]]).astype(np.float32)
    both = np.stack([right, right.T])
    hi = both.astype(jnp.bfloat16)
    lo = (both - hi.astype(np.float32)).astype(jnp.bfloat16)
    return np.stack([hi, lo], 1)


def split(x):
    hi = x.astype(jnp.bfloat16)
    lo = (x - hi.astype(jnp.float32)).astype(jnp.bfloat16)
    return hi, lo


def dot(a, b):
    return jnp.dot(a, b, preferred_element_type=jnp.float32)


def right_stage(rows_hi, rows_lo, tab, inv):
    th, tl = tab[inv, 0], tab[inv, 1]
    return dot(rows_hi, th) + dot(rows_lo, th) + dot(rows_hi, tl)


def left_stage(b_hi, b_lo, tab, inv):
    th, tl = tab[1 - inv, 0], tab[1 - inv, 1]
    return dot(th, b_hi) + dot(tl, b_hi) + dot(th, b_lo)


def to_pairs(y, G):
    out = []
    for p in range(0, G, 2):
        two = [y[j * W:(j + 1) * W] for j in range(p, min(p + 2, G))]
        real = jnp.concatenate([v[:, :W] for v in two], 1)
        imag = jnp.concatenate([v[:, W:] for v in two], 1)
        out.append(jnp.concatenate([real, imag], 0))
    return out


def from_pairs(bs):
    rows = []
    for z in bs:
        for k in range(z.shape[1] // W):
            rows.append(jnp.concatenate([z[:W, k * W:(k + 1) * W], z[W:, k * W:(k + 1) * W]], 1))
    return jnp.concatenate(rows, 0)


def sandwich(load, store, G, tab, mid):
    def enter(p, v):
        x = jnp.concatenate([load(j) for j in range(2 * p, min(2 * p + 2, G))], 0)
        return split(to_pairs(right_stage(*split(x), tab, 0), x.shape[0] // W)[0])

    def middle(p, v):
        z = left_stage(*v, tab, 0)
        zr, zi = mid(p, z[:W], z[W:])
        return split(jnp.concatenate([zr, zi], 0))

    def back(p, v):
        return split(from_pairs([left_stage(*v, tab, 1)]))

    def leave(p, v):
        store(p, right_stage(*v, tab, 1))

    pairs = (G + 1) // 2
    state = [None] * pairs
    for stage in (enter, middle, back, leave):
        for p in range(pairs):
            state[p] = stage(p, state[p])


def cut(obj, s, comp, R, C):
    blk = jnp.minimum(C // W, 2)
    sh = C - blk * W
    turn = (W - sh) % W
    left = pltpu.roll(obj[s, comp, blk, pl.ds(R, W), :], turn, 1)
    right = pltpu.roll(obj[s, comp, blk + 1, pl.ds(R, W), :], turn, 1)
    lane = lax.broadcasted_iota(jnp.int32, (W, W), 1)
    return jnp.where(lane < W - sh, left, right)


def put(acc, s, comp, R, C, g):
    blk = jnp.minimum(C // W, 2)
    sh = C - blk * W
    turned = pltpu.roll(g, sh % W, 1)
    lane = lax.broadcasted_iota(jnp.int32, (W, W), 1)
    la = (s, comp, blk, pl.ds(R, W), slice(None))
    lb = (s, comp, blk + 1, pl.ds(R, W), slice(None))
    acc[la] = acc[la] + jnp.where(lane >= sh, turned, 0.0)
    acc[lb] = acc[lb] + jnp.where(lane < sh, turned, 0.0)


def plan(place, mine, prev, offs, cols, srcs):
    d, t, last = place[0], place[1], place[2]
    stays = [(q < mine[16]) & ((mine[q] <= HALF) | (t == last)) for q in range(8)]
    comes = [(q < prev[16]) & (prev[q] > HALF) for q in range(8)]
    one = [jnp.where(c, 1, 0) for c in stays]
    two = [jnp.where(c, 1, 0) for c in comes]
    own = sum(one)
    x0 = sum(two[0::2])
    x1 = sum(two[1::2])
    a0 = jnp.clip((own + x0 + x1 + 1) // 2 - x0, 0, own)
    low = jnp.where(d == 0, 0, a0)
    high = jnp.where(d == 0, a0, own)
    n = jnp.int32(0)
    for q in range(8):
        take = comes[q] & (d == q % 2)

        @pl.when(take)
        def _(q=q, n=n):
            offs[n] = prev[q] - HALF
            cols[n] = prev[8 + q]
            srcs[n] = 8 + q // 2

        n = n + jnp.where(take, 1, 0)
    rank = jnp.int32(0)
    for q in range(8):
        take = stays[q] & (rank >= low) & (rank < high)

        @pl.when(take)
        def _(q=q, n=n):
            offs[n] = mine[q] + HALF
            cols[n] = mine[8 + q]
            srcs[n] = q

        n = n + jnp.where(take, 1, 0)
        rank = rank + one[q]
    return n


class Step:
    def __init__(self, G, first, n, lists, obj, hist, H, tab, acc=None):
        offs, cols, srcs = lists
        idx = [jnp.minimum(first + j, n - 1) for j in range(G)]
        self.G, self.first, self.n = G, first, n
        self.R = [offs[i] for i in idx]
        self.C = [cols[i] for i in idx]
        self.I = [srcs[i] for i in idx]
        self.obj, self.hist, self.H, self.tab, self.acc = obj, hist, H, tab, acc

    def rows(self, k, j):
        return self.hist[k, j * W:(j + 1) * W, :W], self.hist[k, j * W:(j + 1) * W, W:]

    def patch(self, s, j):
        return (
            cut(self.obj, s, 0, self.R[j], self.C[j]),
            cut(self.obj, s, 1, self.R[j], self.C[j]),
        )

    def phi(self, s):
        def one(j):
            pr, pi = self.rows(s, j)
            qr, qi = self.patch(s, j)
            return jnp.concatenate([pr * qr - pi * qi, pr * qi + pi * qr], 1)

        return one

    def scatter(self, s, j):
        er, ei = self.rows(GROUP, j)
        pr, pi = self.rows(s, j)

        @pl.when(self.first + j < self.n)
        def _():
            put(self.acc, s, 0, self.R[j], self.C[j], pr * er + pi * ei)
            put(self.acc, s, 1, self.R[j], self.C[j], pr * ei - pi * er)

    def emit(self, s):
        def one(j):
            self.scatter(s, j)
            er, ei = self.rows(GROUP, j)
            qr, qi = self.patch(s, j)
            return jnp.concatenate([qr * er + qi * ei, qr * ei - qi * er], 1)

        return one

    def keep(self, k):
        def one(p, v):
            self.hist[k, 2 * p * W:2 * p * W + v.shape[0], :] = v

        return one

    def times_h(self, sign):
        def mid(p, zr, zi):
            wide = zr.shape[1] // W
            hr = jnp.concatenate([self.H[0]] * wide, 1)
            hi = jnp.concatenate([self.H[1]] * wide, 1) * sign
            return zr * hr - zi * hi, zr * hi + zi * hr

        return mid

    def forward(self, s):
        sandwich(self.phi(s), self.keep(s + 1), self.G, self.tab, self.times_h(1.0))

    def backward(self, s):
        sandwich(self.emit(s), self.keep(GROUP), self.G, self.tab, self.times_h(-1.0))

    def detector(self, inten):
        def chi(p, zr, zi):
            meas = jnp.concatenate([inten[i] for i in self.I[2 * p:2 * p + 2]], 1)
            ex = zr * zr + zi * zi - meas
            return zr * ex, zi * ex

        sandwich(self.phi(GROUP - 1), self.keep(GROUP), self.G, self.tab, chi)


def fetch(d, owner, local, remote, obj, sem):
    waits = []
    for k, (row, rows) in enumerate(SPANS):
        for cb in range(BLOCKS):
            to = obj.at[:, :, cb, pl.ds(row, rows), :]
            one = sem.at[len(waits)]
            here = pltpu.make_async_copy(local[k].at[:, :, :, pl.ds(cb * W, W)], to, one)
            there = pltpu.make_async_copy(remote[k].at[:, :, :, pl.ds(cb * W, W)], to, one)
            pl.when(d == owner)(here.start)
            pl.when(d != owner)(there.start)
            waits.append(here)
    obj[:, :, :, 256:, :] = jnp.zeros((GROUP, 2, BLOCKS, TALL - 256, W), jnp.float32)
    return waits


def deliver(acc, outs, sem):
    copies = []
    for k, (row, rows) in enumerate(SPANS):
        for cb in range(BLOCKS):
            copies.append(
                pltpu.make_async_copy(
                    acc.at[:, :, cb, pl.ds(row, rows), :],
                    outs[k].at[:, :, :, pl.ds(cb * W, W)],
                    sem.at[len(copies)],
                )
            )
            copies[-1].start()
    for c in copies:
        c.wait()


def groups(n, work):
    def body(first):
        left = n - first
        size = jnp.where(left == SIZES[1], SIZES[1], SIZES[0])
        for G in SIZES:
            pl.when(size == G)(lambda G=G: work(G, first))
        return first + size

    lax.while_loop(lambda first: first < n, body, jnp.int32(0))


def first_kernel(place, mine, prev, *refs):
    local, remote = refs[0:3], refs[3:6]
    probe, H, tab, psi = refs[6:10]
    obj, hist, sem, more = refs[10:14]
    lists = refs[14:]
    waits = fetch(place[0], 0, local, remote, obj, sem)
    n = plan(place, mine, prev, *lists)
    for c in waits:
        c.wait()

    def work(G, first):
        step = Step(G, first, n, lists, obj, hist, H, tab)
        hist[0, :G * W, :] = jnp.concatenate([jnp.concatenate([probe[0], probe[1]], 1)] * G, 0)

        def save(s):
            return pltpu.make_async_copy(
                hist.at[s + 1, pl.ds(0, G * W)], psi.at[s, pl.ds(first * W, G * W)], more.at[s]
            )

        def one(s, _):
            step.forward(s)
            save(s).start()
            return 0

        lax.fori_loop(0, GROUP, one, 0)
        for s in range(GROUP):
            save(s).wait()

    groups(n, work)


def second_kernel(place, mine, prev, *refs):
    local, remote = refs[0:3], refs[3:6]
    psi, own_int, got_int, H, tab = refs[6:11]
    outs, err = refs[11:14], refs[14]
    obj, acc, hist, inten, sem, more = refs[15:21]
    lists = refs[21:]
    waits = fetch(place[0], 1, local, remote, obj, sem)
    for k, (a, b) in enumerate(
        ((own_int, inten.at[pl.ds(0, 8)]), (got_int, inten.at[pl.ds(8, 4)]))
    ):
        waits.append(pltpu.make_async_copy(a, b, more.at[k]))
        waits[-1].start()
    n = plan(place, mine, prev, *lists)
    acc[...] = jnp.zeros_like(acc)
    for c in waits:
        c.wait()

    def work(G, first):
        step = Step(G, first, n, lists, obj, hist, H, tab, acc)
        at = pl.ds(first * W, G * W)
        load = pltpu.make_async_copy(psi.at[GROUP - 1, at], hist.at[0, pl.ds(0, G * W)], more.at[2])
        load.start()
        load.wait()

        def ahead(s, _):
            step.forward(s)
            return 0

        lax.fori_loop(0, GROUP - 1, ahead, 0)
        step.detector(inten)

        def back(k, _):
            step.backward(GROUP - 1 - k)
            return 0

        lax.fori_loop(0, GROUP, back, 0)
        save = pltpu.make_async_copy(hist.at[GROUP, pl.ds(0, G * W)], err.at[at], more.at[3])
        save.start()
        save.wait()

    groups(n, work)
    deliver(acc, outs, sem)


def third_kernel(place, mine, prev, *refs):
    local, remote = refs[0:3], refs[3:6]
    psi, err, probe, H, tab = refs[6:11]
    outs = refs[11:14]
    obj, acc, hist, sem, more = refs[14:19]
    lists = refs[19:]
    waits = fetch(place[0], 0, local, remote, obj, sem)
    n = plan(place, mine, prev, *lists)
    acc[...] = jnp.zeros_like(acc)
    for c in waits:
        c.wait()

    def work(G, first):
        step = Step(G, first, n, lists, obj, hist, H, tab, acc)
        at = pl.ds(first * W, G * W)
        loads = [
            pltpu.make_async_copy(err.at[at], hist.at[GROUP, pl.ds(0, G * W)], more.at[0])
        ] + [
            pltpu.make_async_copy(psi.at[s - 1, at], hist.at[s, pl.ds(0, G * W)], more.at[s])
            for s in range(1, GROUP)
        ]
        for c in loads:
            c.start()
        hist[0, :G * W, :] = jnp.concatenate([jnp.concatenate([probe[0], probe[1]], 1)] * G, 0)
        for c in loads:
            c.wait()

        def back(k, _):
            step.backward(GROUP - 1 - k)
            return 0

        lax.fori_loop(0, GROUP - 1, back, 0)
        for j in range(G):
            step.scatter(0, j)

    groups(n, work)
    deliver(acc, outs, sem)


def between(value, by, depth):
    count = lax.axis_size("tile")
    steps = [(i, i + by) for i in range(count) if 0 <= i + by < count]
    if depth is None:
        return lax.ppermute(value, "tile", steps)
    pairs = [(depth * count + a, depth * count + b) for a, b in steps]
    return lax.ppermute(value, ("depth", "tile"), pairs)


def across(value, pairs):
    return lax.ppermute(value, "depth", pairs)


def local(
    specimen_layers,
    illumination_field,
    propagator_spectral_angle,
    recorded_intensities,
    patch_upper_edges,
    patch_left_edges,
    occupied_places_per_band,
):
    depth = lax.axis_index("depth")
    tile = lax.axis_index("tile")
    columns = specimen_layers.shape[3]
    place = jnp.stack([depth, tile, jnp.int32(lax.axis_size("tile") - 1)]).astype(jnp.int32)
    mine = jnp.concatenate([patch_upper_edges, patch_left_edges, occupied_places_per_band])
    prev = between(mine, 1, None)
    top = specimen_layers[:, :, :HALF]
    bottom = specimen_layers[:, :, HALF:]
    low_next = between(top, -1, 0)
    low_prev = between(bottom, 1, 0)
    other = across(specimen_layers, [(0, 1), (1, 0)])
    other_low_next = across(low_next, [(0, 1)])
    other_low_prev = across(low_prev, [(0, 1)])
    high_next = between(top, -1, 1)
    high_prev = between(bottom, 1, 1)
    sent_int = lax.dynamic_index_in_dim(
        recorded_intensities.reshape(4, 2, W, W), depth, 1, keepdims=False
    )
    got_int = between(sent_int, 1, None)
    other_high_next = across(high_next, [(1, 0)])
    other_high_prev = across(high_prev, [(1, 0)])
    H = jnp.stack([jnp.cos(propagator_spectral_angle), jnp.sin(propagator_spectral_angle)])
    tab = jnp.asarray(tables())
    hbm = pl.BlockSpec(memory_space=pl.ANY)
    vm = pl.BlockSpec(memory_space=pltpu.VMEM)
    sm = pl.BlockSpec(memory_space=pltpu.SMEM)
    parts = [jax.ShapeDtypeStruct((GROUP, 2, rows, columns), jnp.float32) for row, rows in SPANS]
    waves = jax.ShapeDtypeStruct((GROUP, ROOM * W, 2 * W), jnp.float32)
    errors = jax.ShapeDtypeStruct((ROOM * W, 2 * W), jnp.float32)
    field = pltpu.VMEM((GROUP, 2, BLOCKS, TALL, W), jnp.float32)
    hist = pltpu.VMEM((GROUP + 1, SIZES[1] * W, 2 * W), jnp.float32)
    sems = [pltpu.SemaphoreType.DMA((12,)), pltpu.SemaphoreType.DMA((4,))]
    lists = [pltpu.SMEM((8,), jnp.int32)] * 3
    params = pltpu.CompilerParams(vmem_limit_bytes=56 * 1024 * 1024)
    where = (place, mine, prev)
    psi = pl.pallas_call(
        first_kernel,
        out_shape=waves,
        in_specs=[sm] * 3 + [hbm] * 6 + [vm] * 3,
        out_specs=hbm,
        scratch_shapes=[field, hist] + sems + lists,
        compiler_params=params,
        name="first",
    )(
        *where, low_prev, specimen_layers, low_next, other_low_prev, other, other_low_next,
        illumination_field, H, tab,
    )
    h_prev, h_own, h_next, err = pl.pallas_call(
        second_kernel,
        out_shape=parts + [errors],
        in_specs=[sm] * 3 + [hbm] * 9 + [vm] * 2,
        out_specs=[hbm] * 4,
        scratch_shapes=[field, field, hist, pltpu.VMEM((12, W, W), jnp.float32)] + sems + lists,
        compiler_params=params,
        name="second",
    )(
        *where, high_prev, specimen_layers, high_next, other_high_prev, other, other_high_next,
        psi, recorded_intensities, got_int, H, tab,
    )
    high_up = h_prev + across(h_prev, [(0, 1)])
    high_down = h_next + across(h_next, [(0, 1)])
    high_from_next = between(high_up, -1, 1)
    high_from_prev = between(high_down, 1, 1)
    other_h_own = across(h_own, [(0, 1)])
    l_prev, l_own, l_next = pl.pallas_call(
        third_kernel,
        out_shape=parts,
        in_specs=[sm] * 3 + [hbm] * 8 + [vm] * 3,
        out_specs=[hbm] * 3,
        scratch_shapes=[field, field, hist] + sems + lists,
        compiler_params=params,
        name="third",
    )(
        *where, low_prev, specimen_layers, low_next, other_low_prev, other, other_low_next,
        psi, err, illumination_field, H, tab,
    )
    low_up = l_prev + across(l_prev, [(1, 0)])
    low_down = l_next + across(l_next, [(1, 0)])
    low_from_next = between(low_up, -1, 0)
    low_from_prev = between(low_down, 1, 0)
    other_l_own = across(l_own, [(1, 0)])
    partial = (
        jnp.where(depth == 0, l_own, h_own)
        + jnp.where(depth == 0, other_l_own, other_h_own)
        + jnp.concatenate([high_from_prev, high_from_next], axis=2)
    )
    partial = lax.optimization_barrier(partial)
    return partial + jnp.concatenate([low_from_prev, low_from_next], axis=2)


def solution(mesh):
    placed = (
        P("depth", None, "tile", None),
        P(),
        P(),
        P("tile", None, None),
        P("tile"),
        P("tile"),
        P("tile"),
    )
    return jax.shard_map(
        local, mesh=mesh, in_specs=placed, out_specs=P("depth", None, "tile", None), check_vma=False
    )
```

```python
import math

import jax
import jax.numpy as jnp
import numpy as np
from jax import lax
from jax.experimental import pallas as pl
from jax.experimental.pallas import tpu as pltpu
from jax.sharding import PartitionSpec as P


W = 128
S = 8
RIM = 72
INTS = 16
TALL = 256
BLOCKS = 4
SLOTS = 8
SIZES = (4, 6, 8)

def tables():
    k = np.arange(W)
    a = (k[:, None] * k[None, :] % W) * (2 * math.pi / W)
    cr = np.cos(a) / math.sqrt(W)
    ci = -np.sin(a) / math.sqrt(W)
    right = np.block([[cr, ci], [-ci, cr]]).astype(np.float32)
    both = np.stack([right, right.T])
    hi = both.astype(jnp.bfloat16)
    lo = (both - hi.astype(np.float32)).astype(jnp.bfloat16)
    return np.stack([hi, lo], 1)

def split(x):
    hi = x.astype(jnp.bfloat16)
    lo = (x - hi.astype(jnp.float32)).astype(jnp.bfloat16)
    return hi, lo

def dot(a, b):
    return jnp.dot(a, b, preferred_element_type=jnp.float32)

def right_stage(rows_hi, rows_lo, tab, inv):
    th, tl = tab[inv, 0], tab[inv, 1]
    return dot(rows_hi, th) + dot(rows_lo, th) + dot(rows_hi, tl)

def left_stage(b_hi, b_lo, tab, inv):
    th, tl = tab[1 - inv, 0], tab[1 - inv, 1]
    return dot(th, b_hi) + dot(tl, b_hi) + dot(th, b_lo)

def to_pairs(y, G):
    out = []
    for p in range(0, G, 2):
        two = [y[j * W:(j + 1) * W] for j in range(p, min(p + 2, G))]
        real = jnp.concatenate([v[:, :W] for v in two], 1)
        imag = jnp.concatenate([v[:, W:] for v in two], 1)
        out.append(jnp.concatenate([real, imag], 0))
    return out


def from_pairs(bs):
    rows = []
    for z in bs:
        for k in range(z.shape[1] // W):
            rows.append(jnp.concatenate([z[:W, k * W:(k + 1) * W], z[W:, k * W:(k + 1) * W]], 1))
    return jnp.concatenate(rows, 0)


def sandwich(load, store, G, tab, mid):
    def enter(p, v):
        x = jnp.concatenate([load(j) for j in range(2 * p, min(2 * p + 2, G))], 0)
        return split(to_pairs(right_stage(*split(x), tab, 0), x.shape[0] // W)[0])

    def middle(p, v):
        z = left_stage(*v, tab, 0)
        zr, zi = mid(p, z[:W], z[W:])
        return split(jnp.concatenate([zr, zi], 0))

    def back(p, v):
        return split(from_pairs([left_stage(*v, tab, 1)]))

    def leave(p, v):
        store(p, right_stage(*v, tab, 1))

    pairs = (G + 1) // 2
    state = [None] * pairs
    for stage in (enter, middle, back, leave):
        for p in range(pairs):
            state[p] = stage(p, state[p])


def cut(obj, s, comp, R, C):
    blk = jnp.minimum(C // W, 2)
    sh = C - blk * W
    turn = (W - sh) % W
    left = pltpu.roll(obj[s, comp, blk, pl.ds(R, W), :], turn, 1)
    right = pltpu.roll(obj[s, comp, blk + 1, pl.ds(R, W), :], turn, 1)
    lane = lax.broadcasted_iota(jnp.int32, (W, W), 1)
    return jnp.where(lane < W - sh, left, right)


def put(acc, s, comp, R, C, g):
    blk = jnp.minimum(C // W, 2)
    sh = C - blk * W
    turned = pltpu.roll(g, sh % W, 1)
    lane = lax.broadcasted_iota(jnp.int32, (W, W), 1)
    la = (s, comp, blk, pl.ds(R, W), slice(None))
    lb = (s, comp, blk + 1, pl.ds(R, W), slice(None))
    acc[la] = acc[la] + jnp.where(lane >= sh, turned, 0.0)
    acc[lb] = acc[lb] + jnp.where(lane < sh, turned, 0.0)


class Step:
    def __init__(self, G, n, lists, obj, hist, H, tab, acc=None):
        offs, cols, srcs = lists
        idx = [jnp.maximum(jnp.minimum(j, n - 1), 0) for j in range(G)]
        self.G, self.n = G, n
        self.R = [offs[i] for i in idx]
        self.C = [cols[i] for i in idx]
        self.I = [srcs[i] for i in idx]
        self.obj, self.hist, self.H, self.tab, self.acc = obj, hist, H, tab, acc

    def rows(self, k, j):
        return self.hist[k, j * W:(j + 1) * W, :W], self.hist[k, j * W:(j + 1) * W, W:]

    def patch(self, s, j):
        return (
            cut(self.obj, s, 0, self.R[j], self.C[j]),
            cut(self.obj, s, 1, self.R[j], self.C[j]),
        )

    def phi(self, s):
        def one(j):
            pr, pi = self.rows(s, j)
            qr, qi = self.patch(s, j)
            return jnp.concatenate([pr * qr - pi * qi, pr * qi + pi * qr], 1)

        return one

    def scatter(self, s, j):
        er, ei = self.rows(S, j)
        pr, pi = self.rows(s, j)

        @pl.when(j < self.n)
        def _():
            put(self.acc, s, 0, self.R[j], self.C[j], pr * er + pi * ei)
            put(self.acc, s, 1, self.R[j], self.C[j], pr * ei - pi * er)

    def emit(self, s):
        def one(j):
            self.scatter(s, j)
            er, ei = self.rows(S, j)
            qr, qi = self.patch(s, j)
            return jnp.concatenate([qr * er + qi * ei, qr * ei - qi * er], 1)

        return one

    def keep(self, k):
        def one(p, v):
            self.hist[k, 2 * p * W:2 * p * W + v.shape[0], :] = v

        return one

    def times_h(self, sign):
        def mid(p, zr, zi):
            wide = zr.shape[1] // W
            hr = jnp.concatenate([self.H[0]] * wide, 1)
            hi = jnp.concatenate([self.H[1]] * wide, 1) * sign
            return zr * hr - zi * hi, zr * hi + zi * hr

        return mid

    def forward(self, s):
        sandwich(self.phi(s), self.keep(s + 1), self.G, self.tab, self.times_h(1.0))

    def backward(self, s):
        sandwich(self.emit(s), self.keep(S), self.G, self.tab, self.times_h(-1.0))

    def detector(self, inten):
        def chi(p, zr, zi):
            meas = jnp.concatenate(
                [inten[i].reshape(W, W) for i in self.I[2 * p:2 * p + 2]], 1
            )
            ex = zr * zr + zi * zi - meas
            return zr * ex, zi * ex

        sandwich(self.phi(S - 1), self.keep(S), self.G, self.tab, chi)


def plan(place, mine, prev, offs, cols, srcs):
    d, t, last = place[0], place[1], place[2]
    for q in range(SLOTS):
        offs[q] = 0
        cols[q] = 0
        srcs[q] = 0
    n = jnp.int32(0)
    for q in range(SLOTS):
        stays = (q < mine[16]) & ((mine[q] <= RIM) | (t == last))
        comes = (q < prev[16]) & (prev[q] > RIM)
        take = jnp.where(d == 0, stays, comes)

        @pl.when(take)
        def _(q=q, n=n):
            offs[n] = jnp.where(d == 0, mine[q], prev[q] - RIM + INTS)
            cols[n] = jnp.where(d == 0, mine[8 + q], prev[8 + q])
            srcs[n] = q

        n = n + jnp.where(take, 1, 0)
    return n


def main_kernel(
    place, mine, prev, my_own, my_rim, other_own, other_rim, ints, probe, H, tab,
    out_own, out_own_other, out_rim, out_rim_other,
    obj, acc, hist, inten, offs, cols, srcs, sem, isem,
):
    d = place[0]
    own_row = pl.multiple_of(jnp.where(d == 0, 0, RIM), 8)
    rim_row = pl.multiple_of(jnp.where(d == 0, W, 0), 8)

    def moves(s, i, own, rim, field, out):
        pairs = []
        for cb in range(BLOCKS):
            for k, (far, row, rows) in enumerate(((own, own_row, W), (rim, rim_row, RIM))):
                a = far.at[i, :, :, pl.ds(cb * W, W)]
                b = field.at[s, :, cb, pl.ds(row, rows), :]
                a, b = (b, a) if out else (a, b)
                pairs.append(pltpu.make_async_copy(a, b, sem.at[s, 2 * cb + k]))
        return pairs

    def start_in(i, _):
        for c in moves(d * 4 + i, i, my_own, my_rim, obj, False):
            c.start()
        for c in moves((1 - d) * 4 + i, i, other_own, other_rim, obj, False):
            c.start()
        return 0

    lax.fori_loop(0, S // 2, start_in, 0)

    def near(q):
        return pltpu.make_async_copy(ints.at[q], inten.at[q], isem.at[q])

    def far(q, rim):
        return [
            pltpu.make_async_copy(
                rim.at[i, c, pl.ds(0, INTS), pl.ds((q % 4) * W, W)],
                inten.at[q, 2 * i + c],
                isem.at[8 + q * 8 + 2 * i + c],
            )
            for i in range(4) for c in range(2)
        ]

    def each(act):
        @pl.when(d == 0)
        def _():
            for q in range(SLOTS):
                act(near(q))

        @pl.when(d == 1)
        def _():
            for q in range(SLOTS):
                for c in far(q, my_rim if q < 4 else other_rim):
                    act(c)

    each(lambda c: c.start())
    n = plan(place, mine, prev, offs, cols, srcs)
    obj[:, :, :, W + RIM:, :] = jnp.zeros((S, 2, BLOCKS, TALL - W - RIM, W), jnp.float32)

    def work(G):
        step = Step(G, n, (offs, cols, srcs), obj, hist, H, tab, acc)
        hist[0, :G * W, :] = jnp.concatenate([jnp.concatenate([probe[0], probe[1]], 1)] * G, 0)

        def arrive(s):
            for c in moves(s, 0, my_own, my_rim, obj, False):
                c.wait()

        def ahead(s, _):
            arrive(s)
            step.forward(s)
            return 0

        lax.fori_loop(0, S - 1, ahead, 0)
        arrive(S - 1)
        each(lambda c: c.wait())
        step.detector(inten)

        def send(s):
            @pl.when(s // 4 == d)
            def _():
                for c in moves(s, s % 4, out_own, out_rim, acc, True):
                    c.start()

            @pl.when(s // 4 != d)
            def _():
                for c in moves(s, s % 4, out_own_other, out_rim_other, acc, True):
                    c.start()

        def clear(s):
            acc[s] = jnp.zeros((2, BLOCKS, TALL, W), jnp.float32)

        def back(k, _):
            s = S - 1 - k
            clear(s)
            step.backward(s)
            send(s)
            return 0

        lax.fori_loop(0, S - 1, back, 0)
        clear(0)
        for j in range(G):
            step.scatter(0, j)
        send(jnp.int32(0))

    least = 0
    for G in SIZES:
        pl.when((n >= least) & (n <= G))(lambda G=G: work(G))
        least = G + 1

    def gone(s, _):
        for c in moves(s, 0, out_own, out_rim, acc, True):
            c.wait()
        return 0

    lax.fori_loop(0, S, gone, 0)


def both_ways(value, outward):
    count = lax.axis_size("tile")
    up = [(i, i - 1) for i in range(1, count)]
    down = [(i, i + 1) for i in range(count - 1)]
    first, second = (down, up) if outward else (up, down)
    pairs = first + [(count + a, count + b) for a, b in second]
    return lax.ppermute(value, ("depth", "tile"), pairs)


def partner(value):
    return lax.ppermute(value, "depth", [(0, 1), (1, 0)])


def packed(depth, field, ints):
    side = ints.reshape(4, 4, 2, INTS, W).transpose(1, 2, 3, 0, 4).reshape(4, 2, INTS, 4 * W)
    below = jnp.concatenate([side, field[:, :, RIM:]], axis=2)
    return jnp.where(depth == 0, field[:, :, :RIM], below)


def local(
    specimen_layers,
    illumination_field,
    propagator_spectral_angle,
    recorded_intensities,
    patch_upper_edges,
    patch_left_edges,
    occupied_places_per_band,
):
    depth = lax.axis_index("depth")
    tile = lax.axis_index("tile")
    columns = specimen_layers.shape[3]
    count = lax.axis_size("tile")
    place = jnp.stack([depth, tile, jnp.int32(count - 1)]).astype(jnp.int32)
    mine = jnp.concatenate([patch_upper_edges, patch_left_edges, occupied_places_per_band])
    with jax.named_scope("meta"):
        prev = lax.ppermute(mine, "tile", [(i, i + 1) for i in range(count - 1)])
    with jax.named_scope("own"):
        other = partner(specimen_layers)
    with jax.named_scope("rim1"):
        my_rim = both_ways(packed(depth, specimen_layers, recorded_intensities[:4]), False)
    with jax.named_scope("rim2"):
        other_rim = both_ways(packed(depth, other, recorded_intensities[4:]), False)
    H = jnp.stack([jnp.cos(propagator_spectral_angle), jnp.sin(propagator_spectral_angle)])
    hbm = pl.BlockSpec(memory_space=pl.ANY)
    vm = pl.BlockSpec(memory_space=pltpu.VMEM)
    sm = pl.BlockSpec(memory_space=pltpu.SMEM)
    own = jax.ShapeDtypeStruct((4, 2, W, columns), jnp.float32)
    rim = jax.ShapeDtypeStruct((4, 2, RIM, columns), jnp.float32)
    field = pltpu.VMEM((S, 2, BLOCKS, TALL, W), jnp.float32)
    g_own, g_own_other, g_rim, g_rim_other = pl.pallas_call(
        main_kernel,
        out_shape=[own, own, rim, rim],
        in_specs=[sm] * 3 + [hbm] * 5 + [vm] * 3,
        out_specs=[hbm] * 4,
        scratch_shapes=[
            field,
            field,
            pltpu.VMEM((S + 1, SLOTS * W, 2 * W), jnp.float32),
            pltpu.VMEM((SLOTS, 8, INTS, W), jnp.float32),
            pltpu.SMEM((SLOTS,), jnp.int32),
            pltpu.SMEM((SLOTS,), jnp.int32),
            pltpu.SMEM((SLOTS,), jnp.int32),
            pltpu.SemaphoreType.DMA((S, 2 * BLOCKS)),
            pltpu.SemaphoreType.DMA((72,)),
        ],
        compiler_params=pltpu.CompilerParams(vmem_limit_bytes=56 * 1024 * 1024),
        name="slots",
    )(
        place, mine, prev, specimen_layers, my_rim, other, other_rim,
        recorded_intensities.reshape(SLOTS, 8, INTS, W), illumination_field, H,
        jnp.asarray(tables()),
    )
    with jax.named_scope("out1"):
        came_other = both_ways(g_rim_other, True)
    with jax.named_scope("out2"):
        came = both_ways(g_rim, True)
    with jax.named_scope("out3"):
        own_other = partner(g_own_other)
    with jax.named_scope("out4"):
        crossed = partner(came_other)
    head = jnp.where(depth == 0, came, crossed)
    foot = jnp.where(depth == 0, crossed, came)
    return g_own + own_other + jnp.concatenate([head, foot[:, :, INTS:]], axis=2)


def solution(mesh):
    placed = (
        P("depth", None, "tile", None),
        P(),
        P(),
        P("tile", None, None),
        P("tile"),
        P("tile"),
        P("tile"),
    )
    return jax.shard_map(
        local, mesh=mesh, in_specs=placed, out_specs=P("depth", None, "tile", None), check_vma=False
    )
```

```python
import math

import jax
import jax.numpy as jnp
import numpy as np
from jax import lax
from jax.experimental import pallas as pl
from jax.experimental.pallas import tpu as pltpu
from jax.sharding import PartitionSpec as P


W = 128
S = 8
RIM = 72
INTS = 16
TALL = 256
BLOCKS = 4
SLOTS = 8
SIZES = (4, 6, 8)

def tables():
    k = np.arange(W)
    a = (k[:, None] * k[None, :] % W) * (2 * math.pi / W)
    cr = np.cos(a) / math.sqrt(W)
    ci = -np.sin(a) / math.sqrt(W)
    right = np.block([[cr, ci], [-ci, cr]]).astype(np.float32)
    both = np.stack([right, right.T])
    hi = both.astype(jnp.bfloat16)
    lo = (both - hi.astype(np.float32)).astype(jnp.bfloat16)
    return np.stack([hi, lo], 1)

def split(x):
    hi = x.astype(jnp.bfloat16)
    lo = (x - hi.astype(jnp.float32)).astype(jnp.bfloat16)
    return hi, lo

def dot(a, b):
    return jnp.dot(a, b, preferred_element_type=jnp.float32)

def right_stage(rows_hi, rows_lo, tab, inv):
    th, tl = tab[inv, 0], tab[inv, 1]
    return dot(rows_hi, th) + dot(rows_lo, th) + dot(rows_hi, tl)

def left_stage(b_hi, b_lo, tab, inv):
    th, tl = tab[1 - inv, 0], tab[1 - inv, 1]
    return dot(th, b_hi) + dot(tl, b_hi) + dot(th, b_lo)

def to_pairs(y, G):
    out = []
    for p in range(0, G, 2):
        two = [y[j * W:(j + 1) * W] for j in range(p, min(p + 2, G))]
        real = jnp.concatenate([v[:, :W] for v in two], 1)
        imag = jnp.concatenate([v[:, W:] for v in two], 1)
        out.append(jnp.concatenate([real, imag], 0))
    return out


def from_pairs(bs):
    rows = []
    for z in bs:
        for k in range(z.shape[1] // W):
            rows.append(jnp.concatenate([z[:W, k * W:(k + 1) * W], z[W:, k * W:(k + 1) * W]], 1))
    return jnp.concatenate(rows, 0)


def sandwich(load, store, G, tab, mid):
    def enter(p, v):
        x = jnp.concatenate([load(j) for j in range(2 * p, min(2 * p + 2, G))], 0)
        return split(to_pairs(right_stage(*split(x), tab, 0), x.shape[0] // W)[0])

    def middle(p, v):
        z = left_stage(*v, tab, 0)
        zr, zi = mid(p, z[:W], z[W:])
        return split(jnp.concatenate([zr, zi], 0))

    def back(p, v):
        return split(from_pairs([left_stage(*v, tab, 1)]))

    def leave(p, v):
        store(p, right_stage(*v, tab, 1))

    pairs = (G + 1) // 2
    state = [None] * pairs
    for stage in (enter, middle, back, leave):
        for p in range(pairs):
            state[p] = stage(p, state[p])


def cut(obj, s, comp, R, C):
    blk = jnp.minimum(C // W, 2)
    sh = C - blk * W
    turn = (W - sh) % W
    left = pltpu.roll(obj[s, comp, blk, pl.ds(R, W), :], turn, 1)
    right = pltpu.roll(obj[s, comp, blk + 1, pl.ds(R, W), :], turn, 1)
    lane = lax.broadcasted_iota(jnp.int32, (W, W), 1)
    return jnp.where(lane < W - sh, left, right)


def put(acc, s, comp, R, C, g, live):
    blk = jnp.minimum(C // W, 2)
    sh = C - blk * W
    turned = pltpu.roll(g, sh % W, 1)
    lane = lax.broadcasted_iota(jnp.int32, (W, W), 1)
    la = (s, comp, blk, pl.ds(R, W), slice(None))
    lb = (s, comp, blk + 1, pl.ds(R, W), slice(None))
    acc[la] = acc[la] + jnp.where(lane >= jnp.where(live, sh, W), turned, 0.0)
    acc[lb] = acc[lb] + jnp.where(lane < jnp.where(live, sh, 0), turned, 0.0)


class Step:
    def __init__(self, G, n, lists, obj, hist, H, tab, acc=None):
        offs, cols, srcs = lists
        idx = [jnp.maximum(jnp.minimum(j, n - 1), 0) for j in range(G)]
        self.G, self.n = G, n
        self.R = [offs[i] for i in idx]
        self.C = [cols[i] for i in idx]
        self.I = [srcs[i] for i in idx]
        self.obj, self.hist, self.H, self.tab, self.acc = obj, hist, H, tab, acc

    def rows(self, k, j):
        return self.hist[k, j * W:(j + 1) * W, :W], self.hist[k, j * W:(j + 1) * W, W:]

    def patch(self, s, j):
        return (
            cut(self.obj, s, 0, self.R[j], self.C[j]),
            cut(self.obj, s, 1, self.R[j], self.C[j]),
        )

    def phi(self, s):
        def one(j):
            pr, pi = self.rows(s, j)
            qr, qi = self.patch(s, j)
            return jnp.concatenate([pr * qr - pi * qi, pr * qi + pi * qr], 1)

        return one

    def scatter(self, s, j):
        er, ei = self.rows(S, j)
        pr, pi = self.rows(s, j)
        live = j < self.n
        put(self.acc, s, 0, self.R[j], self.C[j], pr * er + pi * ei, live)
        put(self.acc, s, 1, self.R[j], self.C[j], pr * ei - pi * er, live)

    def emit(self, s):
        def one(j):
            self.scatter(s, j)
            er, ei = self.rows(S, j)
            qr, qi = self.patch(s, j)
            return jnp.concatenate([qr * er + qi * ei, qr * ei - qi * er], 1)

        return one

    def keep(self, k):
        def one(p, v):
            self.hist[k, 2 * p * W:2 * p * W + v.shape[0], :] = v

        return one

    def times_h(self, sign):
        def mid(p, zr, zi):
            wide = zr.shape[1] // W
            hr = jnp.concatenate([self.H[0]] * wide, 1)
            hi = jnp.concatenate([self.H[1]] * wide, 1) * sign
            return zr * hr - zi * hi, zr * hi + zi * hr

        return mid

    def forward(self, s):
        sandwich(self.phi(s), self.keep(s + 1), self.G, self.tab, self.times_h(1.0))

    def backward(self, s):
        sandwich(self.emit(s), self.keep(S), self.G, self.tab, self.times_h(-1.0))

    def detector(self, inten):
        def chi(p, zr, zi):
            meas = jnp.concatenate(
                [inten[i].reshape(W, W) for i in self.I[2 * p:2 * p + 2]], 1
            )
            ex = zr * zr + zi * zi - meas
            return zr * ex, zi * ex

        sandwich(self.phi(S - 1), self.keep(S), self.G, self.tab, chi)


def plan(place, mine, prev, offs, cols, srcs):
    d, t, last = place[0], place[1], place[2]
    for q in range(SLOTS):
        offs[q] = 0
        cols[q] = 0
        srcs[q] = 0
    n = jnp.int32(0)
    for q in range(SLOTS):
        stays = (q < mine[16]) & ((mine[q] <= RIM) | (t == last))
        comes = (q < prev[16]) & (prev[q] > RIM)
        take = jnp.where(d == 0, stays, comes)

        @pl.when(take)
        def _(q=q, n=n):
            offs[n] = jnp.where(d == 0, mine[q], prev[q] - RIM + INTS)
            cols[n] = jnp.where(d == 0, mine[8 + q], prev[8 + q])
            srcs[n] = q

        n = n + jnp.where(take, 1, 0)
    return n


def main_kernel(
    place, mine, prev, my_own, my_rim, other_own, other_rim, ints, probe, H, tab,
    out_own, out_own_other, out_rim, out_rim_other,
    obj, acc, hist, inten, offs, cols, srcs, sem, isem,
):
    d = place[0]
    own_row = pl.multiple_of(jnp.where(d == 0, 0, RIM), 8)
    rim_row = pl.multiple_of(jnp.where(d == 0, W, 0), 8)

    def moves(s, i, own, rim, field, out):
        pairs = []
        for cb in range(BLOCKS):
            for k, (far, row, rows) in enumerate(((own, own_row, W), (rim, rim_row, RIM))):
                a = far.at[i, :, :, pl.ds(cb * W, W)]
                b = field.at[s, :, cb, pl.ds(row, rows), :]
                a, b = (b, a) if out else (a, b)
                pairs.append(pltpu.make_async_copy(a, b, sem.at[s, 2 * cb + k]))
        return pairs

    def start_in(i, _):
        for c in moves(d * 4 + i, i, my_own, my_rim, obj, False):
            c.start()
        for c in moves((1 - d) * 4 + i, i, other_own, other_rim, obj, False):
            c.start()
        return 0

    lax.fori_loop(0, S // 2, start_in, 0)

    def near(q):
        return pltpu.make_async_copy(ints.at[q], inten.at[q], isem.at[q])

    def far(q, rim):
        return [
            pltpu.make_async_copy(
                rim.at[i, c, pl.ds(0, INTS), pl.ds((q % 4) * W, W)],
                inten.at[q, 2 * i + c],
                isem.at[8 + q * 8 + 2 * i + c],
            )
            for i in range(4) for c in range(2)
        ]

    def each(act):
        @pl.when(d == 0)
        def _():
            for q in range(SLOTS):
                act(near(q))

        @pl.when(d == 1)
        def _():
            for q in range(SLOTS):
                for c in far(q, my_rim if q < 4 else other_rim):
                    act(c)

    each(lambda c: c.start())
    n = plan(place, mine, prev, offs, cols, srcs)
    obj[:, :, :, W + RIM:, :] = jnp.zeros((S, 2, BLOCKS, TALL - W - RIM, W), jnp.float32)

    def work(G):
        step = Step(G, n, (offs, cols, srcs), obj, hist, H, tab, acc)
        hist[0, :G * W, :] = jnp.concatenate([jnp.concatenate([probe[0], probe[1]], 1)] * G, 0)

        def arrive(s):
            for c in moves(s, 0, my_own, my_rim, obj, False):
                c.wait()

        def ahead(s, _):
            arrive(s)
            step.forward(s)
            return 0

        lax.fori_loop(0, S - 1, ahead, 0)
        arrive(S - 1)
        each(lambda c: c.wait())
        step.detector(inten)

        def send(s):
            @pl.when(s // 4 == d)
            def _():
                for c in moves(s, s % 4, out_own, out_rim, acc, True):
                    c.start()

            @pl.when(s // 4 != d)
            def _():
                for c in moves(s, s % 4, out_own_other, out_rim_other, acc, True):
                    c.start()

        def clear(s):
            acc[s] = jnp.zeros((2, BLOCKS, TALL, W), jnp.float32)

        def back(k, _):
            s = S - 1 - k
            clear(s)
            step.backward(s)
            send(s)
            return 0

        lax.fori_loop(0, S - 1, back, 0)
        clear(0)
        for j in range(G):
            step.scatter(0, j)
        send(jnp.int32(0))

    least = 0
    for G in SIZES:
        pl.when((n >= least) & (n <= G))(lambda G=G: work(G))
        least = G + 1

    def gone(s, _):
        for c in moves(s, 0, out_own, out_rim, acc, True):
            c.wait()
        return 0

    lax.fori_loop(0, S, gone, 0)


def both_ways(value, outward):
    count = lax.axis_size("tile")
    up = [(i, i - 1) for i in range(1, count)]
    down = [(i, i + 1) for i in range(count - 1)]
    first, second = (down, up) if outward else (up, down)
    pairs = first + [(count + a, count + b) for a, b in second]
    return lax.ppermute(value, ("depth", "tile"), pairs)


def partner(value):
    return lax.ppermute(value, "depth", [(0, 1), (1, 0)])


def packed(depth, field, ints):
    side = ints.reshape(4, 4, 2, INTS, W).transpose(1, 2, 3, 0, 4).reshape(4, 2, INTS, 4 * W)
    below = jnp.concatenate([side, field[:, :, RIM:]], axis=2)
    return jnp.where(depth == 0, field[:, :, :RIM], below)


def local(
    specimen_layers,
    illumination_field,
    propagator_spectral_angle,
    recorded_intensities,
    patch_upper_edges,
    patch_left_edges,
    occupied_places_per_band,
):
    depth = lax.axis_index("depth")
    tile = lax.axis_index("tile")
    columns = specimen_layers.shape[3]
    count = lax.axis_size("tile")
    place = jnp.stack([depth, tile, jnp.int32(count - 1)]).astype(jnp.int32)
    mine = jnp.concatenate([patch_upper_edges, patch_left_edges, occupied_places_per_band])
    with jax.named_scope("meta"):
        prev = lax.ppermute(mine, "tile", [(i, i + 1) for i in range(count - 1)])
    with jax.named_scope("own"):
        other = partner(specimen_layers)
    with jax.named_scope("rim1"):
        my_rim = both_ways(packed(depth, specimen_layers, recorded_intensities[:4]), False)
    with jax.named_scope("rim2"):
        other_rim = both_ways(packed(depth, other, recorded_intensities[4:]), False)
    H = jnp.stack([jnp.cos(propagator_spectral_angle), jnp.sin(propagator_spectral_angle)])
    hbm = pl.BlockSpec(memory_space=pl.ANY)
    vm = pl.BlockSpec(memory_space=pltpu.VMEM)
    sm = pl.BlockSpec(memory_space=pltpu.SMEM)
    own = jax.ShapeDtypeStruct((4, 2, W, columns), jnp.float32)
    rim = jax.ShapeDtypeStruct((4, 2, RIM, columns), jnp.float32)
    field = pltpu.VMEM((S, 2, BLOCKS, TALL, W), jnp.float32)
    g_own, g_own_other, g_rim, g_rim_other = pl.pallas_call(
        main_kernel,
        out_shape=[own, own, rim, rim],
        in_specs=[sm] * 3 + [hbm] * 5 + [vm] * 3,
        out_specs=[hbm] * 4,
        scratch_shapes=[
            field,
            field,
            pltpu.VMEM((S + 1, SLOTS * W, 2 * W), jnp.float32),
            pltpu.VMEM((SLOTS, 8, INTS, W), jnp.float32),
            pltpu.SMEM((SLOTS,), jnp.int32),
            pltpu.SMEM((SLOTS,), jnp.int32),
            pltpu.SMEM((SLOTS,), jnp.int32),
            pltpu.SemaphoreType.DMA((S, 2 * BLOCKS)),
            pltpu.SemaphoreType.DMA((72,)),
        ],
        compiler_params=pltpu.CompilerParams(vmem_limit_bytes=56 * 1024 * 1024),
        name="slots",
    )(
        place, mine, prev, specimen_layers, my_rim, other, other_rim,
        recorded_intensities.reshape(SLOTS, 8, INTS, W), illumination_field, H,
        jnp.asarray(tables()),
    )
    with jax.named_scope("out1"):
        came_other = both_ways(g_rim_other, True)
    with jax.named_scope("out2"):
        came = both_ways(g_rim, True)
    with jax.named_scope("out3"):
        own_other = partner(g_own_other)
    with jax.named_scope("out4"):
        crossed = partner(came_other)
    head = jnp.where(depth == 0, came, crossed)
    foot = jnp.where(depth == 0, crossed, came)
    return g_own + own_other + jnp.concatenate([head, foot[:, :, INTS:]], axis=2)


def solution(mesh):
    placed = (
        P("depth", None, "tile", None),
        P(),
        P(),
        P("tile", None, None),
        P("tile"),
        P("tile"),
        P("tile"),
    )
    return jax.shard_map(
        local, mesh=mesh, in_specs=placed, out_specs=P("depth", None, "tile", None), check_vma=False
    )
```

```python
import math

import jax
import jax.numpy as jnp
import numpy as np
from jax import lax
from jax.experimental import pallas as pl
from jax.experimental.pallas import tpu as pltpu
from jax.sharding import PartitionSpec as P


W = 128
RIM = 72
INTS = 16
TALL = 256
BLOCKS = 4
SLOTS = 8
SIZES = (6, 8)
GROUP = 4


def tables():
    k = np.arange(W)
    a = (k[:, None] * k[None, :] % W) * (2 * math.pi / W)
    cr = np.cos(a) / math.sqrt(W)
    ci = -np.sin(a) / math.sqrt(W)
    right = np.block([[cr, ci], [-ci, cr]]).astype(np.float32)
    both = np.stack([right, right.T])
    hi = both.astype(jnp.bfloat16)
    lo = (both - hi.astype(np.float32)).astype(jnp.bfloat16)
    return np.stack([hi, lo], 1)


def split(x):
    hi = x.astype(jnp.bfloat16)
    lo = (x - hi.astype(jnp.float32)).astype(jnp.bfloat16)
    return hi, lo


def dot(a, b):
    return jnp.dot(a, b, preferred_element_type=jnp.float32)


def right_stage(rows_hi, rows_lo, tab, inv):
    th, tl = tab[inv, 0], tab[inv, 1]
    return dot(rows_hi, th) + dot(rows_lo, th) + dot(rows_hi, tl)


def left_stage(b_hi, b_lo, tab, inv):
    th, tl = tab[1 - inv, 0], tab[1 - inv, 1]
    return dot(th, b_hi) + dot(tl, b_hi) + dot(th, b_lo)


def to_pairs(y, G):
    out = []
    for p in range(0, G, 2):
        two = [y[j * W:(j + 1) * W] for j in range(p, min(p + 2, G))]
        real = jnp.concatenate([v[:, :W] for v in two], 1)
        imag = jnp.concatenate([v[:, W:] for v in two], 1)
        out.append(jnp.concatenate([real, imag], 0))
    return out


def from_pairs(bs):
    rows = []
    for z in bs:
        for k in range(z.shape[1] // W):
            rows.append(jnp.concatenate([z[:W, k * W:(k + 1) * W], z[W:, k * W:(k + 1) * W]], 1))
    return jnp.concatenate(rows, 0)


def sandwich(load, store, G, tab, mid):
    def enter(p, v):
        x = jnp.concatenate([load(j) for j in range(2 * p, min(2 * p + 2, G))], 0)
        return split(to_pairs(right_stage(*split(x), tab, 0), x.shape[0] // W)[0])

    def middle(p, v):
        z = left_stage(*v, tab, 0)
        zr, zi = mid(p, z[:W], z[W:])
        return split(jnp.concatenate([zr, zi], 0))

    def back(p, v):
        return split(from_pairs([left_stage(*v, tab, 1)]))

    def leave(p, v):
        store(p, right_stage(*v, tab, 1))

    pairs = (G + 1) // 2
    state = [None] * pairs
    for stage in (enter, middle, back, leave):
        for p in range(pairs):
            state[p] = stage(p, state[p])


def cut(obj, s, comp, R, C):
    blk = jnp.minimum(C // W, 2)
    sh = C - blk * W
    turn = (W - sh) % W
    left = pltpu.roll(obj[s, comp, blk, pl.ds(R, W), :], turn, 1)
    right = pltpu.roll(obj[s, comp, blk + 1, pl.ds(R, W), :], turn, 1)
    lane = lax.broadcasted_iota(jnp.int32, (W, W), 1)
    return jnp.where(lane < W - sh, left, right)


def put(acc, s, comp, R, C, g, live):
    blk = jnp.minimum(C // W, 2)
    sh = C - blk * W
    turned = pltpu.roll(g, sh % W, 1)
    lane = lax.broadcasted_iota(jnp.int32, (W, W), 1)
    la = (s, comp, blk, pl.ds(R, W), slice(None))
    lb = (s, comp, blk + 1, pl.ds(R, W), slice(None))
    acc[la] = acc[la] + jnp.where(lane >= jnp.where(live, sh, W), turned, 0.0)
    acc[lb] = acc[lb] + jnp.where(lane < jnp.where(live, sh, 0), turned, 0.0)


class Step:
    def __init__(self, G, n, lists, obj, hist, H, tab, acc=None):
        offs, cols, srcs = lists
        idx = [jnp.maximum(jnp.minimum(j, n - 1), 0) for j in range(G)]
        self.G, self.n = G, n
        self.R = [offs[i] for i in idx]
        self.C = [cols[i] for i in idx]
        self.I = [srcs[i] for i in idx]
        self.obj, self.hist, self.H, self.tab, self.acc = obj, hist, H, tab, acc

    def rows(self, k, j):
        return self.hist[k, j * W:(j + 1) * W, :W], self.hist[k, j * W:(j + 1) * W, W:]

    def patch(self, s, j):
        return (
            cut(self.obj, s, 0, self.R[j], self.C[j]),
            cut(self.obj, s, 1, self.R[j], self.C[j]),
        )

    def phi(self, s):
        def one(j):
            pr, pi = self.rows(s, j)
            qr, qi = self.patch(s, j)
            return jnp.concatenate([pr * qr - pi * qi, pr * qi + pi * qr], 1)

        return one

    def scatter(self, s, j):
        er, ei = self.rows(GROUP, j)
        pr, pi = self.rows(s, j)
        live = j < self.n
        put(self.acc, s, 0, self.R[j], self.C[j], pr * er + pi * ei, live)
        put(self.acc, s, 1, self.R[j], self.C[j], pr * ei - pi * er, live)

    def emit(self, s):
        def one(j):
            self.scatter(s, j)
            er, ei = self.rows(GROUP, j)
            qr, qi = self.patch(s, j)
            return jnp.concatenate([qr * er + qi * ei, qr * ei - qi * er], 1)

        return one

    def keep(self, k):
        def one(p, v):
            self.hist[k, 2 * p * W:2 * p * W + v.shape[0], :] = v

        return one

    def times_h(self, sign):
        def mid(p, zr, zi):
            wide = zr.shape[1] // W
            hr = jnp.concatenate([self.H[0]] * wide, 1)
            hi = jnp.concatenate([self.H[1]] * wide, 1) * sign
            return zr * hr - zi * hi, zr * hi + zi * hr

        return mid

    def forward(self, s):
        sandwich(self.phi(s), self.keep(s + 1), self.G, self.tab, self.times_h(1.0))

    def backward(self, s):
        sandwich(self.emit(s), self.keep(GROUP), self.G, self.tab, self.times_h(-1.0))

    def detector(self, inten):
        def chi(p, zr, zi):
            meas = jnp.concatenate(
                [inten[i].reshape(W, W) for i in self.I[2 * p:2 * p + 2]], 1
            )
            ex = zr * zr + zi * zi - meas
            return zr * ex, zi * ex

        sandwich(self.phi(GROUP - 1), self.keep(GROUP), self.G, self.tab, chi)


def plan(place, mine, prev, offs, cols, srcs):
    d, t, last = place[0], place[1], place[2]
    for q in range(SLOTS):
        offs[q] = 0
        cols[q] = 0
        srcs[q] = 0
    n = jnp.int32(0)
    for q in range(SLOTS):
        stays = (q < mine[16]) & ((mine[q] <= RIM) | (t == last))
        comes = (q < prev[16]) & (prev[q] > RIM)
        take = jnp.where(d == 0, stays, comes)

        @pl.when(take)
        def _(q=q, n=n):
            offs[n] = jnp.where(d == 0, mine[q], prev[q] - RIM + INTS)
            cols[n] = jnp.where(d == 0, mine[8 + q], prev[8 + q])
            srcs[n] = q

        n = n + jnp.where(take, 1, 0)
    return n


class Core:
    def __init__(self, place, sem):
        self.d, self.sem = place[0], sem
        self.own_row = pl.multiple_of(jnp.where(self.d == 0, 0, RIM), 8)
        self.rim_row = pl.multiple_of(jnp.where(self.d == 0, W, 0), 8)

    def moves(self, s, own, rim, field, out):
        pairs = []
        for cb in range(BLOCKS):
            for k, (far, row, rows) in enumerate(
                ((own, self.own_row, W), (rim, self.rim_row, RIM))
            ):
                a = far.at[s, :, :, pl.ds(cb * W, W)]
                b = field.at[s, :, cb, pl.ds(row, rows), :]
                a, b = (b, a) if out else (a, b)
                pairs.append(pltpu.make_async_copy(a, b, self.sem.at[s, 2 * cb + k]))
        return pairs

    def fetch(self, owner, mine, other, rim, obj, downward=False):
        def one(i, _):
            s = GROUP - 1 - i if downward else i

            @pl.when(self.d == owner)
            def _():
                for c in self.moves(s, mine, rim, obj, False):
                    c.start()

            @pl.when(self.d != owner)
            def _():
                for c in self.moves(s, other, rim, obj, False):
                    c.start()

            return 0

        lax.fori_loop(0, GROUP, one, 0)

    def arrive(self, s, mine, rim, obj):
        for c in self.moves(s, mine, rim, obj, False):
            c.wait()

    def send(self, s, own, rim, acc):
        for c in self.moves(s, own, rim, acc, True):
            c.start()

    def gone(self, own, rim, acc):
        def one(s, _):
            for c in self.moves(s, own, rim, acc, True):
                c.wait()
            return 0

        lax.fori_loop(0, GROUP, one, 0)


def blank(obj):
    obj[:, :, :, W + RIM:, :] = jnp.zeros((GROUP, 2, BLOCKS, TALL - W - RIM, W), jnp.float32)


def clear(acc, s):
    acc[s] = jnp.zeros((2, BLOCKS, TALL, W), jnp.float32)


def sized(n, work):
    pl.when(n <= SIZES[0])(lambda: work(SIZES[0]))
    pl.when(n > SIZES[0])(lambda: work(SIZES[1]))


def first_kernel(
    place, mine, prev, my_own, other_own, rim, probe, H, tab, psi,
    obj, hist, offs, cols, srcs, sem, more,
):
    core = Core(place, sem)
    core.fetch(0, my_own, other_own, rim, obj)
    n = plan(place, mine, prev, offs, cols, srcs)
    blank(obj)

    def save(s):
        return pltpu.make_async_copy(hist.at[s + 1], psi.at[s], more.at[s])

    def work(G):
        step = Step(G, n, (offs, cols, srcs), obj, hist, H, tab)
        hist[0, :G * W, :] = jnp.concatenate([jnp.concatenate([probe[0], probe[1]], 1)] * G, 0)

        def ahead(s, _):
            core.arrive(s, my_own, rim, obj)
            step.forward(s)
            save(s).start()
            return 0

        lax.fori_loop(0, GROUP, ahead, 0)

    sized(n, work)
    for s in range(GROUP):
        save(s).wait()


def second_kernel(
    place, mine, prev, my_own, other_own, rim, low_rim, psi, ints, H, tab,
    out_own, out_rim, err,
    obj, acc, hist, inten, offs, cols, srcs, sem, more, isem,
):
    core = Core(place, sem)
    start = pltpu.make_async_copy(psi.at[GROUP - 1], hist.at[0], more.at[0])
    start.start()
    core.fetch(1, my_own, other_own, rim, obj)

    def near(q):
        return pltpu.make_async_copy(ints.at[q], inten.at[q], isem.at[q])

    def far(q, source):
        return [
            pltpu.make_async_copy(
                source.at[i, c, pl.ds(0, INTS), pl.ds((q % 4) * W, W)],
                inten.at[q, 2 * i + c],
                isem.at[8 + q * 8 + 2 * i + c],
            )
            for i in range(4) for c in range(2)
        ]

    def each(act):
        @pl.when(core.d == 0)
        def _():
            for q in range(SLOTS):
                act(near(q))

        @pl.when(core.d == 1)
        def _():
            for q in range(SLOTS):
                for c in far(q, low_rim if q < 4 else rim):
                    act(c)

    each(lambda c: c.start())
    n = plan(place, mine, prev, offs, cols, srcs)
    blank(obj)
    start.wait()

    def work(G):
        step = Step(G, n, (offs, cols, srcs), obj, hist, H, tab, acc)

        def ahead(s, _):
            core.arrive(s, my_own, rim, obj)
            step.forward(s)
            return 0

        lax.fori_loop(0, GROUP - 1, ahead, 0)
        core.arrive(GROUP - 1, my_own, rim, obj)
        each(lambda c: c.wait())
        step.detector(inten)

        def back(k, _):
            s = GROUP - 1 - k
            clear(acc, s)
            step.backward(s)
            core.send(s, out_own, out_rim, acc)
            return 0

        lax.fori_loop(0, GROUP, back, 0)

    sized(n, work)
    end = pltpu.make_async_copy(hist.at[GROUP], err, more.at[1])
    end.start()
    core.gone(out_own, out_rim, acc)
    end.wait()


def third_kernel(
    place, mine, prev, my_own, other_own, rim, psi, err, probe, H, tab,
    out_own, out_rim,
    obj, acc, hist, offs, cols, srcs, sem, more,
):
    core = Core(place, sem)

    def load(s):
        return pltpu.make_async_copy(psi.at[s - 1], hist.at[s], more.at[s])

    start = pltpu.make_async_copy(err, hist.at[GROUP], more.at[0])
    start.start()
    load(GROUP - 1).start()
    core.fetch(0, my_own, other_own, rim, obj, True)
    for s in range(GROUP - 2, 0, -1):
        load(s).start()
    n = plan(place, mine, prev, offs, cols, srcs)
    blank(obj)
    start.wait()

    def work(G):
        step = Step(G, n, (offs, cols, srcs), obj, hist, H, tab, acc)
        hist[0, :G * W, :] = jnp.concatenate([jnp.concatenate([probe[0], probe[1]], 1)] * G, 0)

        def back(k, _):
            s = GROUP - 1 - k
            clear(acc, s)
            load(s).wait()
            core.arrive(s, my_own, rim, obj)
            step.backward(s)
            core.send(s, out_own, out_rim, acc)
            return 0

        lax.fori_loop(0, GROUP - 1, back, 0)
        core.arrive(0, my_own, rim, obj)
        clear(acc, 0)
        for j in range(G):
            step.scatter(0, j)
        core.send(0, out_own, out_rim, acc)

    sized(n, work)
    core.gone(out_own, out_rim, acc)


def both_ways(value, outward):
    count = lax.axis_size("tile")
    up = [(i, i - 1) for i in range(1, count)]
    down = [(i, i + 1) for i in range(count - 1)]
    first, second = (down, up) if outward else (up, down)
    pairs = first + [(count + a, count + b) for a, b in second]
    return lax.ppermute(value, ("depth", "tile"), pairs)


def partner(value):
    return lax.ppermute(value, "depth", [(0, 1), (1, 0)])


def packed(depth, above, below, ints):
    side = ints.reshape(4, 4, 2, INTS, W).transpose(1, 2, 3, 0, 4).reshape(4, 2, INTS, 4 * W)
    return jnp.where(
        depth == 0, above[:, :, :RIM], jnp.concatenate([side, below[:, :, RIM:]], axis=2)
    )


def local(
    specimen_layers,
    illumination_field,
    propagator_spectral_angle,
    recorded_intensities,
    patch_upper_edges,
    patch_left_edges,
    occupied_places_per_band,
):
    depth = lax.axis_index("depth")
    tile = lax.axis_index("tile")
    columns = specimen_layers.shape[3]
    count = lax.axis_size("tile")
    place = jnp.stack([depth, tile, jnp.int32(count - 1)]).astype(jnp.int32)
    mine = jnp.concatenate([patch_upper_edges, patch_left_edges, occupied_places_per_band])
    other = partner(specimen_layers)
    prev = lax.ppermute(
        mine, ("depth", "tile"), [(count + i, count + i + 1) for i in range(count - 1)]
    )
    low = packed(depth, specimen_layers, other, recorded_intensities[:4])
    high = packed(depth, other, specimen_layers, recorded_intensities[4:])
    low_rim = both_ways(low, False)
    high_rim = both_ways(high, False)
    H = jnp.stack([jnp.cos(propagator_spectral_angle), jnp.sin(propagator_spectral_angle)])
    tab = jnp.asarray(tables())
    hbm = pl.BlockSpec(memory_space=pl.ANY)
    vm = pl.BlockSpec(memory_space=pltpu.VMEM)
    sm = pl.BlockSpec(memory_space=pltpu.SMEM)
    own = jax.ShapeDtypeStruct((GROUP, 2, W, columns), jnp.float32)
    rim = jax.ShapeDtypeStruct((GROUP, 2, RIM, columns), jnp.float32)
    errors = jax.ShapeDtypeStruct((SLOTS * W, 2 * W), jnp.float32)
    field = pltpu.VMEM((GROUP, 2, BLOCKS, TALL, W), jnp.float32)
    hist = pltpu.VMEM((GROUP + 1, SLOTS * W, 2 * W), jnp.float32)
    tail = [pltpu.SMEM((SLOTS,), jnp.int32)] * 3 + [
        pltpu.SemaphoreType.DMA((GROUP, 2 * BLOCKS)),
        pltpu.SemaphoreType.DMA((GROUP,)),
    ]
    params = pltpu.CompilerParams(vmem_limit_bytes=48 * 1024 * 1024)
    where = (place, mine, prev, specimen_layers, other)
    psi = pl.pallas_call(
        first_kernel,
        out_shape=jax.ShapeDtypeStruct((GROUP, SLOTS * W, 2 * W), jnp.float32),
        in_specs=[sm] * 3 + [hbm] * 3 + [vm] * 3,
        out_specs=hbm,
        scratch_shapes=[field, hist] + tail,
        compiler_params=params,
        name="first",
    )(*where, low_rim, illumination_field, H, tab)
    own_high, rim_high, err = pl.pallas_call(
        second_kernel,
        out_shape=[own, rim, errors],
        in_specs=[sm] * 3 + [hbm] * 6 + [vm] * 2,
        out_specs=[hbm] * 3,
        scratch_shapes=[field, field, hist, pltpu.VMEM((SLOTS, 8, INTS, W), jnp.float32)]
        + tail + [pltpu.SemaphoreType.DMA((72,))],
        compiler_params=params,
        name="second",
    )(
        *where, high_rim, low_rim, psi,
        recorded_intensities.reshape(SLOTS, 8, INTS, W), H, tab,
    )
    came_high = both_ways(rim_high, True)
    own_low, rim_low = pl.pallas_call(
        third_kernel,
        out_shape=[own, rim],
        in_specs=[sm] * 3 + [hbm] * 5 + [vm] * 3,
        out_specs=[hbm] * 2,
        scratch_shapes=[field, field, hist] + tail,
        compiler_params=params,
        name="third",
    )(*where, low_rim, psi, err, illumination_field, H, tab)
    came_low = both_ways(rim_low, True)
    head = jnp.concatenate([came_high, jnp.zeros((GROUP, 2, W - RIM, columns))], axis=2)
    given = jnp.where(depth == 0, own_high + head, own_low)
    taken = partner(given)
    foot = jnp.concatenate([jnp.zeros((GROUP, 2, RIM, columns)), came_high[:, :, INTS:]], axis=2)
    total = jnp.where(depth == 0, own_low, own_high + foot) + taken
    total = lax.optimization_barrier(total)
    crossed = lax.ppermute(came_low, "depth", [(1, 0)])
    late = jnp.concatenate([came_low, crossed[:, :, INTS:]], axis=2)
    return total + jnp.where(depth == 0, late, 0.0)


def solution(mesh):
    placed = (
        P("depth", None, "tile", None),
        P(),
        P(),
        P("tile", None, None),
        P("tile"),
        P("tile"),
        P("tile"),
    )
    return jax.shard_map(
        local, mesh=mesh, in_specs=placed, out_specs=P("depth", None, "tile", None), check_vma=False
    )
```

```python
import math

import jax
import jax.numpy as jnp
import numpy as np
from jax import lax
from jax.experimental import pallas as pl
from jax.experimental.pallas import tpu as pltpu
from jax.sharding import PartitionSpec as P


W = 128
RIM = 72
INTS = 16
TALL = 256
BLOCKS = 4
SLOTS = 8
SIZES = (6, 8)
GROUP = 4


def tables():
    k = np.arange(W)
    a = (k[:, None] * k[None, :] % W) * (2 * math.pi / W)
    cr = np.cos(a) / math.sqrt(W)
    ci = -np.sin(a) / math.sqrt(W)
    right = np.block([[cr, ci], [-ci, cr]]).astype(np.float32)
    both = np.stack([right, right.T])
    hi = both.astype(jnp.bfloat16)
    lo = (both - hi.astype(np.float32)).astype(jnp.bfloat16)
    return np.stack([hi, lo], 1)


def split(x):
    hi = x.astype(jnp.bfloat16)
    lo = (x - hi.astype(jnp.float32)).astype(jnp.bfloat16)
    return hi, lo


def dot(a, b):
    return jnp.dot(a, b, preferred_element_type=jnp.float32)


def right_stage(rows_hi, rows_lo, tab, inv):
    th, tl = tab[inv, 0], tab[inv, 1]
    return dot(rows_hi, th) + dot(rows_lo, th) + dot(rows_hi, tl)


def left_stage(b_hi, b_lo, tab, inv):
    th, tl = tab[1 - inv, 0], tab[1 - inv, 1]
    return dot(th, b_hi) + dot(tl, b_hi) + dot(th, b_lo)


def to_pairs(y, G):
    out = []
    for p in range(0, G, 2):
        two = [y[j * W:(j + 1) * W] for j in range(p, min(p + 2, G))]
        real = jnp.concatenate([v[:, :W] for v in two], 1)
        imag = jnp.concatenate([v[:, W:] for v in two], 1)
        out.append(jnp.concatenate([real, imag], 0))
    return out


def from_pairs(bs):
    rows = []
    for z in bs:
        for k in range(z.shape[1] // W):
            rows.append(jnp.concatenate([z[:W, k * W:(k + 1) * W], z[W:, k * W:(k + 1) * W]], 1))
    return jnp.concatenate(rows, 0)


def sandwich(load, store, G, tab, mid):
    def enter(p, v):
        x = jnp.concatenate([load(j) for j in range(2 * p, min(2 * p + 2, G))], 0)
        return split(to_pairs(right_stage(*split(x), tab, 0), x.shape[0] // W)[0])

    def middle(p, v):
        z = left_stage(*v, tab, 0)
        zr, zi = mid(p, z[:W], z[W:])
        return split(jnp.concatenate([zr, zi], 0))

    def back(p, v):
        return split(from_pairs([left_stage(*v, tab, 1)]))

    def leave(p, v):
        store(p, right_stage(*v, tab, 1))

    pairs = (G + 1) // 2
    state = [None] * pairs
    for stage in (enter, middle, back, leave):
        for p in range(pairs):
            state[p] = stage(p, state[p])


def cut(obj, s, comp, R, C):
    blk = jnp.minimum(C // W, 2)
    sh = C - blk * W
    turn = (W - sh) % W
    left = pltpu.roll(obj[s, comp, blk, pl.ds(R, W), :], turn, 1)
    right = pltpu.roll(obj[s, comp, blk + 1, pl.ds(R, W), :], turn, 1)
    lane = lax.broadcasted_iota(jnp.int32, (W, W), 1)
    return jnp.where(lane < W - sh, left, right)


def put(acc, s, comp, R, C, g, live):
    blk = jnp.minimum(C // W, 2)
    sh = C - blk * W
    turned = pltpu.roll(g, sh % W, 1)
    lane = lax.broadcasted_iota(jnp.int32, (W, W), 1)
    la = (s, comp, blk, pl.ds(R, W), slice(None))
    lb = (s, comp, blk + 1, pl.ds(R, W), slice(None))
    acc[la] = acc[la] + jnp.where(lane >= jnp.where(live, sh, W), turned, 0.0)
    acc[lb] = acc[lb] + jnp.where(lane < jnp.where(live, sh, 0), turned, 0.0)


class Step:
    def __init__(self, G, n, lists, obj, hist, H, tab, acc=None):
        offs, cols, srcs = lists
        idx = [jnp.maximum(jnp.minimum(j, n - 1), 0) for j in range(G)]
        self.G, self.n = G, n
        self.R = [offs[i] for i in idx]
        self.C = [cols[i] for i in idx]
        self.I = [srcs[i] for i in idx]
        self.obj, self.hist, self.H, self.tab, self.acc = obj, hist, H, tab, acc

    def rows(self, k, j):
        return self.hist[k, j * W:(j + 1) * W, :W], self.hist[k, j * W:(j + 1) * W, W:]

    def patch(self, s, j):
        return (
            cut(self.obj, s, 0, self.R[j], self.C[j]),
            cut(self.obj, s, 1, self.R[j], self.C[j]),
        )

    def phi(self, s):
        def one(j):
            pr, pi = self.rows(s, j)
            qr, qi = self.patch(s, j)
            return jnp.concatenate([pr * qr - pi * qi, pr * qi + pi * qr], 1)

        return one

    def scatter(self, s, j):
        er, ei = self.rows(GROUP, j)
        pr, pi = self.rows(s, j)
        live = j < self.n
        put(self.acc, s, 0, self.R[j], self.C[j], pr * er + pi * ei, live)
        put(self.acc, s, 1, self.R[j], self.C[j], pr * ei - pi * er, live)

    def emit(self, s):
        def one(j):
            self.scatter(s, j)
            er, ei = self.rows(GROUP, j)
            qr, qi = self.patch(s, j)
            return jnp.concatenate([qr * er + qi * ei, qr * ei - qi * er], 1)

        return one

    def keep(self, k):
        def one(p, v):
            self.hist[k, 2 * p * W:2 * p * W + v.shape[0], :] = v

        return one

    def times_h(self, sign):
        def mid(p, zr, zi):
            wide = zr.shape[1] // W
            hr = jnp.concatenate([self.H[0]] * wide, 1)
            hi = jnp.concatenate([self.H[1]] * wide, 1) * sign
            return zr * hr - zi * hi, zr * hi + zi * hr

        return mid

    def forward(self, s):
        sandwich(self.phi(s), self.keep(s + 1), self.G, self.tab, self.times_h(1.0))

    def backward(self, s):
        sandwich(self.emit(s), self.keep(GROUP), self.G, self.tab, self.times_h(-1.0))

    def detector(self, inten):
        def chi(p, zr, zi):
            meas = jnp.concatenate(
                [inten[i].reshape(W, W) for i in self.I[2 * p:2 * p + 2]], 1
            )
            ex = zr * zr + zi * zi - meas
            return zr * ex, zi * ex

        sandwich(self.phi(GROUP - 1), self.keep(GROUP), self.G, self.tab, chi)


def plan(place, mine, prev, offs, cols, srcs):
    d, t, last = place[0], place[1], place[2]
    for q in range(SLOTS):
        offs[q] = 0
        cols[q] = 0
        srcs[q] = 0
    n = jnp.int32(0)
    for q in range(SLOTS):
        stays = (q < mine[16]) & ((mine[q] <= RIM) | (t == last))
        comes = (q < prev[16]) & (prev[q] > RIM)
        take = jnp.where(d == 0, stays, comes)

        @pl.when(take)
        def _(q=q, n=n):
            offs[n] = jnp.where(d == 0, mine[q], prev[q] - RIM + INTS)
            cols[n] = jnp.where(d == 0, mine[8 + q], prev[8 + q])
            srcs[n] = q

        n = n + jnp.where(take, 1, 0)
    return n


class Core:
    def __init__(self, place, sem):
        self.d, self.sem = place[0], sem
        self.own_row = pl.multiple_of(jnp.where(self.d == 0, 0, RIM), 8)
        self.rim_row = pl.multiple_of(jnp.where(self.d == 0, W, 0), 8)

    def moves(self, s, own, rim, field, out):
        pairs = []
        for cb in range(BLOCKS):
            for k, (far, row, rows) in enumerate(
                ((own, self.own_row, W), (rim, self.rim_row, RIM))
            ):
                a = far.at[s, :, :, pl.ds(cb * W, W)]
                b = field.at[s, :, cb, pl.ds(row, rows), :]
                a, b = (b, a) if out else (a, b)
                pairs.append(pltpu.make_async_copy(a, b, self.sem.at[s, 2 * cb + k]))
        return pairs

    def fetch(self, owner, mine, other, rims, obj, downward=False):
        def one(i, _):
            s = GROUP - 1 - i if downward else i
            for d in range(2):

                @pl.when(self.d == d)
                def _(d=d):
                    for c in self.moves(s, mine if d == owner else other, rims[d], obj, False):
                        c.start()

            return 0

        lax.fori_loop(0, GROUP, one, 0)

    def arrive(self, s, mine, rims, obj):
        for c in self.moves(s, mine, rims[0], obj, False):
            c.wait()

    def send(self, s, own, rim, acc):
        for c in self.moves(s, own, rim, acc, True):
            c.start()

    def gone(self, own, rim, acc):
        def one(s, _):
            for c in self.moves(s, own, rim, acc, True):
                c.wait()
            return 0

        lax.fori_loop(0, GROUP, one, 0)


def blank(obj):
    obj[:, :, :, W + RIM:, :] = jnp.zeros((GROUP, 2, BLOCKS, TALL - W - RIM, W), jnp.float32)


def clear(acc, s):
    acc[s] = jnp.zeros((2, BLOCKS, TALL, W), jnp.float32)


def sized(n, work):
    pl.when(n <= SIZES[0])(lambda: work(SIZES[0]))
    pl.when(n > SIZES[0])(lambda: work(SIZES[1]))


def first_kernel(
    place, mine, prev, my_own, other_own, rim_a, rim_b, probe, H, tab, psi,
    obj, hist, offs, cols, srcs, sem, more,
):
    core = Core(place, sem)
    rims = (rim_a, rim_b)
    core.fetch(0, my_own, other_own, rims, obj)
    n = plan(place, mine, prev, offs, cols, srcs)
    blank(obj)

    def save(s):
        return pltpu.make_async_copy(hist.at[s + 1], psi.at[s], more.at[s])

    def work(G):
        step = Step(G, n, (offs, cols, srcs), obj, hist, H, tab)
        hist[0, :G * W, :] = jnp.concatenate([jnp.concatenate([probe[0], probe[1]], 1)] * G, 0)

        def ahead(s, _):
            core.arrive(s, my_own, rims, obj)
            step.forward(s)
            save(s).start()
            return 0

        lax.fori_loop(0, GROUP, ahead, 0)

    sized(n, work)
    for s in range(GROUP):
        save(s).wait()


def second_kernel(
    place, mine, prev, my_own, other_own, rim_a, rim_b, low_b, psi, ints, H, tab,
    out_own, out_rim, err,
    obj, acc, hist, inten, offs, cols, srcs, sem, more, isem,
):
    core = Core(place, sem)
    rims = (rim_a, rim_b)
    start = pltpu.make_async_copy(psi.at[GROUP - 1], hist.at[0], more.at[0])
    start.start()
    core.fetch(1, my_own, other_own, rims, obj)

    def near(q):
        return pltpu.make_async_copy(ints.at[q], inten.at[q], isem.at[q])

    def far(q, source):
        return [
            pltpu.make_async_copy(
                source.at[i, c, pl.ds(0, INTS), pl.ds((q % 4) * W, W)],
                inten.at[q, 2 * i + c],
                isem.at[8 + q * 8 + 2 * i + c],
            )
            for i in range(4) for c in range(2)
        ]

    def each(act):
        @pl.when(core.d == 0)
        def _():
            for q in range(SLOTS):
                act(near(q))

        @pl.when(core.d == 1)
        def _():
            for q in range(SLOTS):
                for c in far(q, low_b if q < 4 else rim_b):
                    act(c)

    each(lambda c: c.start())
    n = plan(place, mine, prev, offs, cols, srcs)
    blank(obj)
    start.wait()

    def work(G):
        step = Step(G, n, (offs, cols, srcs), obj, hist, H, tab, acc)

        def ahead(s, _):
            core.arrive(s, my_own, rims, obj)
            step.forward(s)
            return 0

        lax.fori_loop(0, GROUP - 1, ahead, 0)
        core.arrive(GROUP - 1, my_own, rims, obj)
        each(lambda c: c.wait())
        step.detector(inten)

        def back(k, _):
            s = GROUP - 1 - k
            clear(acc, s)
            step.backward(s)
            core.send(s, out_own, out_rim, acc)
            return 0

        lax.fori_loop(0, GROUP, back, 0)

    sized(n, work)
    end = pltpu.make_async_copy(hist.at[GROUP], err, more.at[1])
    end.start()
    core.gone(out_own, out_rim, acc)
    end.wait()


def third_kernel(
    place, mine, prev, my_own, other_own, rim_a, rim_b, psi, err, probe, H, tab,
    out_own, out_rim,
    obj, acc, hist, offs, cols, srcs, sem, more,
):
    core = Core(place, sem)
    rims = (rim_a, rim_b)

    def load(s):
        return pltpu.make_async_copy(psi.at[s - 1], hist.at[s], more.at[s])

    start = pltpu.make_async_copy(err, hist.at[GROUP], more.at[0])
    start.start()
    load(GROUP - 1).start()
    core.fetch(0, my_own, other_own, rims, obj, True)
    for s in range(GROUP - 2, 0, -1):
        load(s).start()
    n = plan(place, mine, prev, offs, cols, srcs)
    blank(obj)
    start.wait()

    def work(G):
        step = Step(G, n, (offs, cols, srcs), obj, hist, H, tab, acc)
        hist[0, :G * W, :] = jnp.concatenate([jnp.concatenate([probe[0], probe[1]], 1)] * G, 0)

        def back(k, _):
            s = GROUP - 1 - k
            clear(acc, s)
            load(s).wait()
            core.arrive(s, my_own, rims, obj)
            step.backward(s)
            core.send(s, out_own, out_rim, acc)
            return 0

        lax.fori_loop(0, GROUP - 1, back, 0)
        core.arrive(0, my_own, rims, obj)
        clear(acc, 0)
        for j in range(G):
            step.scatter(0, j)
        core.send(0, out_own, out_rim, acc)

    sized(n, work)
    core.gone(out_own, out_rim, acc)


def outward(value):
    count = lax.axis_size("tile")
    pairs = [(i, i + 1) for i in range(count - 1)]
    pairs += [(count + i, count + i - 1) for i in range(1, count)]
    return lax.ppermute(value, ("depth", "tile"), pairs)


def partner(value):
    return lax.ppermute(value, "depth", [(0, 1), (1, 0)])


def strips(value, by, source, target):
    count = lax.axis_size("tile")
    steps = [(i, i + by) for i in range(count) if 0 <= i + by < count]
    pairs = [(source * count + a, target * count + b) for a, b in steps]
    return lax.ppermute(value, ("depth", "tile"), pairs)


def local(
    specimen_layers,
    illumination_field,
    propagator_spectral_angle,
    recorded_intensities,
    patch_upper_edges,
    patch_left_edges,
    occupied_places_per_band,
):
    depth = lax.axis_index("depth")
    tile = lax.axis_index("tile")
    columns = specimen_layers.shape[3]
    count = lax.axis_size("tile")
    place = jnp.stack([depth, tile, jnp.int32(count - 1)]).astype(jnp.int32)
    mine = jnp.concatenate([patch_upper_edges, patch_left_edges, occupied_places_per_band])
    other = partner(specimen_layers)
    prev = strips(mine, 1, 1, 1)
    ints = jnp.where(depth == 0, recorded_intensities[:4], recorded_intensities[4:])
    side = ints.reshape(4, 4, 2, INTS, W).transpose(1, 2, 3, 0, 4).reshape(4, 2, INTS, columns)
    top = specimen_layers[:, :, :RIM]
    bottom = jnp.concatenate([side, specimen_layers[:, :, RIM:]], axis=2)
    low_a = strips(top, -1, 0, 0)
    low_b = strips(bottom, 1, 0, 1)
    high_a = strips(top, -1, 1, 0)
    high_b = strips(bottom, 1, 1, 1)
    H = jnp.stack([jnp.cos(propagator_spectral_angle), jnp.sin(propagator_spectral_angle)])
    tab = jnp.asarray(tables())
    hbm = pl.BlockSpec(memory_space=pl.ANY)
    vm = pl.BlockSpec(memory_space=pltpu.VMEM)
    sm = pl.BlockSpec(memory_space=pltpu.SMEM)
    own = jax.ShapeDtypeStruct((GROUP, 2, W, columns), jnp.float32)
    rim = jax.ShapeDtypeStruct((GROUP, 2, RIM, columns), jnp.float32)
    errors = jax.ShapeDtypeStruct((SLOTS * W, 2 * W), jnp.float32)
    field = pltpu.VMEM((GROUP, 2, BLOCKS, TALL, W), jnp.float32)
    hist = pltpu.VMEM((GROUP + 1, SLOTS * W, 2 * W), jnp.float32)
    tail = [pltpu.SMEM((SLOTS,), jnp.int32)] * 3 + [
        pltpu.SemaphoreType.DMA((GROUP, 2 * BLOCKS)),
        pltpu.SemaphoreType.DMA((GROUP,)),
    ]
    params = pltpu.CompilerParams(vmem_limit_bytes=48 * 1024 * 1024)
    where = (place, mine, prev, specimen_layers, other)
    psi = pl.pallas_call(
        first_kernel,
        out_shape=jax.ShapeDtypeStruct((GROUP, SLOTS * W, 2 * W), jnp.float32),
        in_specs=[sm] * 3 + [hbm] * 4 + [vm] * 3,
        out_specs=hbm,
        scratch_shapes=[field, hist] + tail,
        compiler_params=params,
        name="first",
    )(*where, low_a, low_b, illumination_field, H, tab)
    own_high, rim_high, err = pl.pallas_call(
        second_kernel,
        out_shape=[own, rim, errors],
        in_specs=[sm] * 3 + [hbm] * 7 + [vm] * 2,
        out_specs=[hbm] * 3,
        scratch_shapes=[field, field, hist, pltpu.VMEM((SLOTS, 8, INTS, W), jnp.float32)]
        + tail + [pltpu.SemaphoreType.DMA((72,))],
        compiler_params=params,
        name="second",
    )(
        *where, high_a, high_b, low_b, psi,
        recorded_intensities.reshape(SLOTS, 8, INTS, W), H, tab,
    )
    came_high = outward(rim_high)
    own_low, rim_low = pl.pallas_call(
        third_kernel,
        out_shape=[own, rim],
        in_specs=[sm] * 3 + [hbm] * 6 + [vm] * 3,
        out_specs=[hbm] * 2,
        scratch_shapes=[field, field, hist] + tail,
        compiler_params=params,
        name="third",
    )(*where, low_a, low_b, psi, err, illumination_field, H, tab)
    low_head = strips(rim_low, 1, 0, 0)
    low_foot = strips(rim_low, -1, 1, 0)
    head = jnp.concatenate([came_high, jnp.zeros((GROUP, 2, W - RIM, columns))], axis=2)
    given = jnp.where(depth == 0, own_high + head, own_low)
    taken = partner(given)
    foot = jnp.concatenate([jnp.zeros((GROUP, 2, RIM, columns)), came_high[:, :, INTS:]], axis=2)
    total = jnp.where(depth == 0, own_low, own_high + foot) + taken
    total = lax.optimization_barrier(total)
    return total + jnp.concatenate([low_head, low_foot[:, :, INTS:]], axis=2)


def solution(mesh):
    placed = (
        P("depth", None, "tile", None),
        P(),
        P(),
        P("tile", None, None),
        P("tile"),
        P("tile"),
        P("tile"),
    )
    return jax.shard_map(
        local, mesh=mesh, in_specs=placed, out_specs=P("depth", None, "tile", None), check_vma=False
    )
```

```python
import math

import jax
import jax.numpy as jnp
import numpy as np
from jax import lax
from jax.experimental import pallas as pl
from jax.experimental.pallas import tpu as pltpu
from jax.sharding import PartitionSpec as P


W = 128
RIM = 72
INTS = 16
TALL = 256
BLOCKS = 4
SLOTS = 8
SIZES = (6, 8)
GROUP = 4


def tables():
    k = np.arange(W)
    a = (k[:, None] * k[None, :] % W) * (2 * math.pi / W)
    cr = np.cos(a) / math.sqrt(W)
    ci = -np.sin(a) / math.sqrt(W)
    right = np.block([[cr, ci], [-ci, cr]]).astype(np.float32)
    both = np.stack([right, right.T])
    hi = both.astype(jnp.bfloat16)
    lo = (both - hi.astype(np.float32)).astype(jnp.bfloat16)
    return np.stack([hi, lo], 1)


def split(x):
    hi = x.astype(jnp.bfloat16)
    lo = (x - hi.astype(jnp.float32)).astype(jnp.bfloat16)
    return hi, lo


def dot(a, b):
    return jnp.dot(a, b, preferred_element_type=jnp.float32)


def right_stage(rows_hi, rows_lo, tab, inv):
    th, tl = tab[inv, 0], tab[inv, 1]
    return dot(rows_hi, th) + dot(rows_lo, th) + dot(rows_hi, tl)


def left_stage(b_hi, b_lo, tab, inv):
    th, tl = tab[1 - inv, 0], tab[1 - inv, 1]
    return dot(th, b_hi) + dot(tl, b_hi) + dot(th, b_lo)


def to_pairs(y, G):
    out = []
    for p in range(0, G, 2):
        two = [y[j * W:(j + 1) * W] for j in range(p, min(p + 2, G))]
        real = jnp.concatenate([v[:, :W] for v in two], 1)
        imag = jnp.concatenate([v[:, W:] for v in two], 1)
        out.append(jnp.concatenate([real, imag], 0))
    return out


def from_pairs(bs):
    rows = []
    for z in bs:
        for k in range(z.shape[1] // W):
            rows.append(jnp.concatenate([z[:W, k * W:(k + 1) * W], z[W:, k * W:(k + 1) * W]], 1))
    return jnp.concatenate(rows, 0)


def sandwich(load, store, G, tab, mid):
    def enter(p, v):
        x = jnp.concatenate([load(j) for j in range(2 * p, min(2 * p + 2, G))], 0)
        return split(to_pairs(right_stage(*split(x), tab, 0), x.shape[0] // W)[0])

    def middle(p, v):
        z = left_stage(*v, tab, 0)
        zr, zi = mid(p, z[:W], z[W:])
        return split(jnp.concatenate([zr, zi], 0))

    def back(p, v):
        return split(from_pairs([left_stage(*v, tab, 1)]))

    def leave(p, v):
        store(p, right_stage(*v, tab, 1))

    pairs = (G + 1) // 2
    state = [None] * pairs
    for stage in (enter, middle, back, leave):
        for p in range(pairs):
            state[p] = stage(p, state[p])


def cut(obj, s, comp, R, C):
    blk = jnp.minimum(C // W, 2)
    sh = C - blk * W
    turn = (W - sh) % W
    left = pltpu.roll(obj[s, comp, blk, pl.ds(R, W), :], turn, 1)
    right = pltpu.roll(obj[s, comp, blk + 1, pl.ds(R, W), :], turn, 1)
    lane = lax.broadcasted_iota(jnp.int32, (W, W), 1)
    return jnp.where(lane < W - sh, left, right)


def put(acc, s, comp, R, C, g, live):
    blk = jnp.minimum(C // W, 2)
    sh = C - blk * W
    turned = pltpu.roll(g, sh % W, 1)
    lane = lax.broadcasted_iota(jnp.int32, (W, W), 1)
    la = (s, comp, blk, pl.ds(R, W), slice(None))
    lb = (s, comp, blk + 1, pl.ds(R, W), slice(None))
    acc[la] = acc[la] + jnp.where(lane >= jnp.where(live, sh, W), turned, 0.0)
    acc[lb] = acc[lb] + jnp.where(lane < jnp.where(live, sh, 0), turned, 0.0)


class Step:
    def __init__(self, G, n, lists, obj, hist, H, tab, acc=None):
        offs, cols, srcs = lists
        idx = [jnp.maximum(jnp.minimum(j, n - 1), 0) for j in range(G)]
        self.G, self.n = G, n
        self.R = [offs[i] for i in idx]
        self.C = [cols[i] for i in idx]
        self.I = [srcs[i] for i in idx]
        self.obj, self.hist, self.H, self.tab, self.acc = obj, hist, H, tab, acc

    def rows(self, k, j):
        return self.hist[k, j * W:(j + 1) * W, :W], self.hist[k, j * W:(j + 1) * W, W:]

    def patch(self, s, j):
        return (
            cut(self.obj, s, 0, self.R[j], self.C[j]),
            cut(self.obj, s, 1, self.R[j], self.C[j]),
        )

    def phi(self, s):
        def one(j):
            pr, pi = self.rows(s, j)
            qr, qi = self.patch(s, j)
            return jnp.concatenate([pr * qr - pi * qi, pr * qi + pi * qr], 1)

        return one

    def scatter(self, s, j):
        er, ei = self.rows(GROUP, j)
        pr, pi = self.rows(s, j)
        live = j < self.n
        put(self.acc, s, 0, self.R[j], self.C[j], pr * er + pi * ei, live)
        put(self.acc, s, 1, self.R[j], self.C[j], pr * ei - pi * er, live)

    def emit(self, s):
        def one(j):
            self.scatter(s, j)
            er, ei = self.rows(GROUP, j)
            qr, qi = self.patch(s, j)
            return jnp.concatenate([qr * er + qi * ei, qr * ei - qi * er], 1)

        return one

    def keep(self, k):
        def one(p, v):
            self.hist[k, 2 * p * W:2 * p * W + v.shape[0], :] = v

        return one

    def times_h(self, sign):
        def mid(p, zr, zi):
            wide = zr.shape[1] // W
            hr = jnp.concatenate([self.H[0]] * wide, 1)
            hi = jnp.concatenate([self.H[1]] * wide, 1) * sign
            return zr * hr - zi * hi, zr * hi + zi * hr

        return mid

    def forward(self, s):
        sandwich(self.phi(s), self.keep(s + 1), self.G, self.tab, self.times_h(1.0))

    def backward(self, s):
        sandwich(self.emit(s), self.keep(GROUP), self.G, self.tab, self.times_h(-1.0))

    def detector(self, inten):
        def chi(p, zr, zi):
            meas = jnp.concatenate(
                [inten[i].reshape(W, W) for i in self.I[2 * p:2 * p + 2]], 1
            )
            ex = zr * zr + zi * zi - meas
            return zr * ex, zi * ex

        sandwich(self.phi(GROUP - 1), self.keep(GROUP), self.G, self.tab, chi)


def plan(place, mine, prev, offs, cols, srcs):
    d, t, last = place[0], place[1], place[2]
    for q in range(SLOTS):
        offs[q] = 0
        cols[q] = 0
        srcs[q] = 0
    n = jnp.int32(0)
    for q in range(SLOTS):
        stays = (q < mine[16]) & ((mine[q] <= RIM) | (t == last))
        comes = (q < prev[16]) & (prev[q] > RIM)
        take = jnp.where(d == 0, stays, comes)

        @pl.when(take)
        def _(q=q, n=n):
            offs[n] = jnp.where(d == 0, mine[q], prev[q] - RIM + INTS)
            cols[n] = jnp.where(d == 0, mine[8 + q], prev[8 + q])
            srcs[n] = q

        n = n + jnp.where(take, 1, 0)
    return n


class Core:
    def __init__(self, place, sem):
        self.d, self.sem = place[0], sem
        self.own_row = pl.multiple_of(jnp.where(self.d == 0, 0, RIM), 8)
        self.rim_row = pl.multiple_of(jnp.where(self.d == 0, W, 0), 8)

    def moves(self, s, own, rim, field, out):
        pairs = []
        for cb in range(BLOCKS):
            for k, (far, row, rows) in enumerate(
                ((own, self.own_row, W), (rim, self.rim_row, RIM))
            ):
                a = far.at[s, :, :, pl.ds(cb * W, W)]
                b = field.at[s, :, cb, pl.ds(row, rows), :]
                a, b = (b, a) if out else (a, b)
                pairs.append(pltpu.make_async_copy(a, b, self.sem.at[s, 2 * cb + k]))
        return pairs

    def fetch(self, owner, mine, other, rim, obj, downward=False):
        def one(i, _):
            s = GROUP - 1 - i if downward else i

            @pl.when(self.d == owner)
            def _():
                for c in self.moves(s, mine, rim, obj, False):
                    c.start()

            @pl.when(self.d != owner)
            def _():
                for c in self.moves(s, other, rim, obj, False):
                    c.start()

            return 0

        lax.fori_loop(0, GROUP, one, 0)

    def arrive(self, s, mine, rim, obj):
        for c in self.moves(s, mine, rim, obj, False):
            c.wait()

    def send(self, s, own, rim, acc):
        for c in self.moves(s, own, rim, acc, True):
            c.start()

    def gone(self, own, rim, acc):
        def one(s, _):
            for c in self.moves(s, own, rim, acc, True):
                c.wait()
            return 0

        lax.fori_loop(0, GROUP, one, 0)


def blank(obj):
    obj[:, :, :, W + RIM:, :] = jnp.zeros((GROUP, 2, BLOCKS, TALL - W - RIM, W), jnp.float32)


def clear(acc, s):
    acc[s] = jnp.zeros((2, BLOCKS, TALL, W), jnp.float32)


def sized(n, work):
    pl.when(n <= SIZES[0])(lambda: work(SIZES[0]))
    pl.when(n > SIZES[0])(lambda: work(SIZES[1]))


def first_kernel(
    place, mine, prev, my_own, other_own, rim, probe, H, tab, psi,
    obj, hist, offs, cols, srcs, sem, more,
):
    core = Core(place, sem)
    core.fetch(0, my_own, other_own, rim, obj)
    n = plan(place, mine, prev, offs, cols, srcs)
    blank(obj)

    def save(s):
        return pltpu.make_async_copy(hist.at[s + 1], psi.at[s], more.at[s])

    def work(G):
        step = Step(G, n, (offs, cols, srcs), obj, hist, H, tab)
        hist[0, :G * W, :] = jnp.concatenate([jnp.concatenate([probe[0], probe[1]], 1)] * G, 0)

        def ahead(s, _):
            core.arrive(s, my_own, rim, obj)
            step.forward(s)
            save(s).start()
            return 0

        lax.fori_loop(0, GROUP, ahead, 0)

    sized(n, work)
    for s in range(GROUP):
        save(s).wait()


def second_kernel(
    place, mine, prev, my_own, other_own, rim, low_rim, psi, ints, H, tab,
    out_own, out_rim, err,
    obj, acc, hist, inten, offs, cols, srcs, sem, more, isem,
):
    core = Core(place, sem)
    start = pltpu.make_async_copy(psi.at[GROUP - 1], hist.at[0], more.at[0])
    start.start()
    core.fetch(1, my_own, other_own, rim, obj)

    def near(q):
        return pltpu.make_async_copy(ints.at[q], inten.at[q], isem.at[q])

    def far(q, source):
        return [
            pltpu.make_async_copy(
                source.at[i, c, pl.ds(0, INTS), pl.ds((q % 4) * W, W)],
                inten.at[q, 2 * i + c],
                isem.at[8 + q * 8 + 2 * i + c],
            )
            for i in range(4) for c in range(2)
        ]

    def each(act):
        @pl.when(core.d == 0)
        def _():
            for q in range(SLOTS):
                act(near(q))

        @pl.when(core.d == 1)
        def _():
            for q in range(SLOTS):
                for c in far(q, low_rim if q < 4 else rim):
                    act(c)

    each(lambda c: c.start())
    n = plan(place, mine, prev, offs, cols, srcs)
    blank(obj)
    start.wait()

    def work(G):
        step = Step(G, n, (offs, cols, srcs), obj, hist, H, tab, acc)

        def ahead(s, _):
            core.arrive(s, my_own, rim, obj)
            step.forward(s)
            return 0

        lax.fori_loop(0, GROUP - 1, ahead, 0)
        core.arrive(GROUP - 1, my_own, rim, obj)
        each(lambda c: c.wait())
        step.detector(inten)

        def back(k, _):
            s = GROUP - 1 - k
            clear(acc, s)
            step.backward(s)
            core.send(s, out_own, out_rim, acc)
            return 0

        lax.fori_loop(0, GROUP, back, 0)

    sized(n, work)
    end = pltpu.make_async_copy(hist.at[GROUP], err, more.at[1])
    end.start()
    core.gone(out_own, out_rim, acc)
    end.wait()


def third_kernel(
    place, mine, prev, my_own, other_own, rim, psi, err, probe, H, tab,
    out_own, out_rim,
    obj, acc, hist, offs, cols, srcs, sem, more,
):
    core = Core(place, sem)

    def load(s):
        return pltpu.make_async_copy(psi.at[s - 1], hist.at[s], more.at[s])

    start = pltpu.make_async_copy(err, hist.at[GROUP], more.at[0])
    start.start()
    load(GROUP - 1).start()
    core.fetch(0, my_own, other_own, rim, obj, True)
    for s in range(GROUP - 2, 0, -1):
        load(s).start()
    n = plan(place, mine, prev, offs, cols, srcs)
    blank(obj)
    start.wait()

    def work(G):
        step = Step(G, n, (offs, cols, srcs), obj, hist, H, tab, acc)
        hist[0, :G * W, :] = jnp.concatenate([jnp.concatenate([probe[0], probe[1]], 1)] * G, 0)

        def back(k, _):
            s = GROUP - 1 - k
            clear(acc, s)
            load(s).wait()
            core.arrive(s, my_own, rim, obj)
            step.backward(s)
            core.send(s, out_own, out_rim, acc)
            return 0

        lax.fori_loop(0, GROUP - 1, back, 0)
        core.arrive(0, my_own, rim, obj)
        clear(acc, 0)
        for j in range(G):
            step.scatter(0, j)
        core.send(0, out_own, out_rim, acc)

    sized(n, work)
    core.gone(out_own, out_rim, acc)


def both_ways(value, outward):
    count = lax.axis_size("tile")
    up = [(i, i - 1) for i in range(1, count)]
    down = [(i, i + 1) for i in range(count - 1)]
    first, second = (down, up) if outward else (up, down)
    pairs = first + [(count + a, count + b) for a, b in second]
    return lax.ppermute(value, ("depth", "tile"), pairs)


def partner(value):
    return lax.ppermute(value, "depth", [(0, 1), (1, 0)])


def strips(value, by, source, target):
    count = lax.axis_size("tile")
    steps = [(i, i + by) for i in range(count) if 0 <= i + by < count]
    pairs = [(source * count + a, target * count + b) for a, b in steps]
    return lax.ppermute(value, ("depth", "tile"), pairs)


def packed(depth, above, below, ints):
    side = ints.reshape(4, 4, 2, INTS, W).transpose(1, 2, 3, 0, 4).reshape(4, 2, INTS, 4 * W)
    return jnp.where(
        depth == 0, above[:, :, :RIM], jnp.concatenate([side, below[:, :, RIM:]], axis=2)
    )


def local(
    specimen_layers,
    illumination_field,
    propagator_spectral_angle,
    recorded_intensities,
    patch_upper_edges,
    patch_left_edges,
    occupied_places_per_band,
):
    depth = lax.axis_index("depth")
    tile = lax.axis_index("tile")
    columns = specimen_layers.shape[3]
    count = lax.axis_size("tile")
    place = jnp.stack([depth, tile, jnp.int32(count - 1)]).astype(jnp.int32)
    mine = jnp.concatenate([patch_upper_edges, patch_left_edges, occupied_places_per_band])
    other = partner(specimen_layers)
    prev = strips(mine, 1, 1, 1)
    low = packed(depth, specimen_layers, other, recorded_intensities[:4])
    high = packed(depth, other, specimen_layers, recorded_intensities[4:])
    low_rim = both_ways(low, False)
    high_rim = both_ways(high, False)
    H = jnp.stack([jnp.cos(propagator_spectral_angle), jnp.sin(propagator_spectral_angle)])
    tab = jnp.asarray(tables())
    hbm = pl.BlockSpec(memory_space=pl.ANY)
    vm = pl.BlockSpec(memory_space=pltpu.VMEM)
    sm = pl.BlockSpec(memory_space=pltpu.SMEM)
    own = jax.ShapeDtypeStruct((GROUP, 2, W, columns), jnp.float32)
    rim = jax.ShapeDtypeStruct((GROUP, 2, RIM, columns), jnp.float32)
    errors = jax.ShapeDtypeStruct((SLOTS * W, 2 * W), jnp.float32)
    field = pltpu.VMEM((GROUP, 2, BLOCKS, TALL, W), jnp.float32)
    hist = pltpu.VMEM((GROUP + 1, SLOTS * W, 2 * W), jnp.float32)
    tail = [pltpu.SMEM((SLOTS,), jnp.int32)] * 3 + [
        pltpu.SemaphoreType.DMA((GROUP, 2 * BLOCKS)),
        pltpu.SemaphoreType.DMA((GROUP,)),
    ]
    params = pltpu.CompilerParams(vmem_limit_bytes=48 * 1024 * 1024)
    where = (place, mine, prev, specimen_layers, other)
    psi = pl.pallas_call(
        first_kernel,
        out_shape=jax.ShapeDtypeStruct((GROUP, SLOTS * W, 2 * W), jnp.float32),
        in_specs=[sm] * 3 + [hbm] * 3 + [vm] * 3,
        out_specs=hbm,
        scratch_shapes=[field, hist] + tail,
        compiler_params=params,
        name="first",
    )(*where, low_rim, illumination_field, H, tab)
    own_high, rim_high, err = pl.pallas_call(
        second_kernel,
        out_shape=[own, rim, errors],
        in_specs=[sm] * 3 + [hbm] * 6 + [vm] * 2,
        out_specs=[hbm] * 3,
        scratch_shapes=[field, field, hist, pltpu.VMEM((SLOTS, 8, INTS, W), jnp.float32)]
        + tail + [pltpu.SemaphoreType.DMA((72,))],
        compiler_params=params,
        name="second",
    )(
        *where, high_rim, low_rim, psi,
        recorded_intensities.reshape(SLOTS, 8, INTS, W), H, tab,
    )
    came_high = both_ways(rim_high, True)
    own_low, rim_low = pl.pallas_call(
        third_kernel,
        out_shape=[own, rim],
        in_specs=[sm] * 3 + [hbm] * 5 + [vm] * 3,
        out_specs=[hbm] * 2,
        scratch_shapes=[field, field, hist] + tail,
        compiler_params=params,
        name="third",
    )(*where, low_rim, psi, err, illumination_field, H, tab)
    low_head = strips(rim_low, 1, 0, 0)
    low_foot = strips(rim_low, -1, 1, 0)
    head = jnp.concatenate([came_high, jnp.zeros((GROUP, 2, W - RIM, columns))], axis=2)
    given = jnp.where(depth == 0, own_high + head, own_low)
    taken = partner(given)
    foot = jnp.concatenate([jnp.zeros((GROUP, 2, RIM, columns)), came_high[:, :, INTS:]], axis=2)
    total = jnp.where(depth == 0, own_low, own_high + foot) + taken
    total = lax.optimization_barrier(total)
    return total + jnp.concatenate([low_head, low_foot[:, :, INTS:]], axis=2)


def solution(mesh):
    placed = (
        P("depth", None, "tile", None),
        P(),
        P(),
        P("tile", None, None),
        P("tile"),
        P("tile"),
        P("tile"),
    )
    return jax.shard_map(
        local, mesh=mesh, in_specs=placed, out_specs=P("depth", None, "tile", None), check_vma=False
    )
```

```python
import math

import jax
import jax.numpy as jnp
import numpy as np
from jax import lax
from jax.experimental import pallas as pl
from jax.experimental.pallas import tpu as pltpu
from jax.sharding import PartitionSpec as P


W = 128
RIM = 72
INTS = 16
TALL = 256
BLOCKS = 4
SLOTS = 8
SIZES = (6, 8)
GROUP = 4


def tables():
    k = np.arange(W)
    a = (k[:, None] * k[None, :] % W) * (2 * math.pi / W)
    cr = np.cos(a) / math.sqrt(W)
    ci = -np.sin(a) / math.sqrt(W)
    right = np.block([[cr, ci], [-ci, cr]]).astype(np.float32)
    both = np.stack([right, right.T])
    hi = both.astype(jnp.bfloat16)
    lo = (both - hi.astype(np.float32)).astype(jnp.bfloat16)
    return np.stack([hi, lo], 1)


def split(x):
    hi = x.astype(jnp.bfloat16)
    lo = (x - hi.astype(jnp.float32)).astype(jnp.bfloat16)
    return hi, lo


def dot(a, b):
    return jnp.dot(a, b, preferred_element_type=jnp.float32)


def right_stage(rows_hi, rows_lo, tab, inv):
    th, tl = tab[inv, 0], tab[inv, 1]
    return dot(rows_hi, th) + dot(rows_lo, th) + dot(rows_hi, tl)


def left_stage(b_hi, b_lo, tab, inv):
    th, tl = tab[1 - inv, 0], tab[1 - inv, 1]
    return dot(th, b_hi) + dot(tl, b_hi) + dot(th, b_lo)


def to_pairs(y, G):
    out = []
    for p in range(0, G, 2):
        two = [y[j * W:(j + 1) * W] for j in range(p, min(p + 2, G))]
        real = jnp.concatenate([v[:, :W] for v in two], 1)
        imag = jnp.concatenate([v[:, W:] for v in two], 1)
        out.append(jnp.concatenate([real, imag], 0))
    return out


def from_pairs(bs):
    rows = []
    for z in bs:
        for k in range(z.shape[1] // W):
            rows.append(jnp.concatenate([z[:W, k * W:(k + 1) * W], z[W:, k * W:(k + 1) * W]], 1))
    return jnp.concatenate(rows, 0)


def sandwich(load, store, G, tab, mid):
    def enter(p, v):
        x = jnp.concatenate([load(j) for j in range(2 * p, min(2 * p + 2, G))], 0)
        return split(to_pairs(right_stage(*split(x), tab, 0), x.shape[0] // W)[0])

    def middle(p, v):
        z = left_stage(*v, tab, 0)
        zr, zi = mid(p, z[:W], z[W:])
        return split(jnp.concatenate([zr, zi], 0))

    def back(p, v):
        return split(from_pairs([left_stage(*v, tab, 1)]))

    def leave(p, v):
        store(p, right_stage(*v, tab, 1))

    pairs = (G + 1) // 2
    state = [None] * pairs
    for stage in (enter, middle, back, leave):
        for p in range(pairs):
            state[p] = stage(p, state[p])


def cut(obj, s, comp, R, C):
    blk = jnp.minimum(C // W, 2)
    sh = C - blk * W
    turn = (W - sh) % W
    left = pltpu.roll(obj[s, comp, blk, pl.ds(R, W), :], turn, 1)
    right = pltpu.roll(obj[s, comp, blk + 1, pl.ds(R, W), :], turn, 1)
    lane = lax.broadcasted_iota(jnp.int32, (W, W), 1)
    return jnp.where(lane < W - sh, left, right)


def put(acc, s, comp, R, C, g, live):
    blk = jnp.minimum(C // W, 2)
    sh = C - blk * W
    turned = pltpu.roll(g, sh % W, 1)
    lane = lax.broadcasted_iota(jnp.int32, (W, W), 1)
    la = (s, comp, blk, pl.ds(R, W), slice(None))
    lb = (s, comp, blk + 1, pl.ds(R, W), slice(None))
    acc[la] = acc[la] + jnp.where(lane >= jnp.where(live, sh, W), turned, 0.0)
    acc[lb] = acc[lb] + jnp.where(lane < jnp.where(live, sh, 0), turned, 0.0)


class Step:
    def __init__(self, G, n, lists, obj, hist, H, tab, acc=None):
        offs, cols, srcs = lists
        idx = [jnp.maximum(jnp.minimum(j, n - 1), 0) for j in range(G)]
        self.G, self.n = G, n
        self.R = [offs[i] for i in idx]
        self.C = [cols[i] for i in idx]
        self.I = [srcs[i] for i in idx]
        self.obj, self.hist, self.H, self.tab, self.acc = obj, hist, H, tab, acc

    def rows(self, k, j):
        return self.hist[k, j * W:(j + 1) * W, :W], self.hist[k, j * W:(j + 1) * W, W:]

    def patch(self, s, j):
        return (
            cut(self.obj, s, 0, self.R[j], self.C[j]),
            cut(self.obj, s, 1, self.R[j], self.C[j]),
        )

    def phi(self, s):
        def one(j):
            pr, pi = self.rows(s, j)
            qr, qi = self.patch(s, j)
            return jnp.concatenate([pr * qr - pi * qi, pr * qi + pi * qr], 1)

        return one

    def scatter(self, s, j):
        er, ei = self.rows(GROUP, j)
        pr, pi = self.rows(s, j)
        live = j < self.n
        put(self.acc, s, 0, self.R[j], self.C[j], pr * er + pi * ei, live)
        put(self.acc, s, 1, self.R[j], self.C[j], pr * ei - pi * er, live)

    def emit(self, s):
        def one(j):
            self.scatter(s, j)
            er, ei = self.rows(GROUP, j)
            qr, qi = self.patch(s, j)
            return jnp.concatenate([qr * er + qi * ei, qr * ei - qi * er], 1)

        return one

    def keep(self, k):
        def one(p, v):
            self.hist[k, 2 * p * W:2 * p * W + v.shape[0], :] = v

        return one

    def times_h(self, sign):
        def mid(p, zr, zi):
            wide = zr.shape[1] // W
            hr = jnp.concatenate([self.H[0]] * wide, 1)
            hi = jnp.concatenate([self.H[1]] * wide, 1) * sign
            return zr * hr - zi * hi, zr * hi + zi * hr

        return mid

    def forward(self, s):
        sandwich(self.phi(s), self.keep(s + 1), self.G, self.tab, self.times_h(1.0))

    def backward(self, s):
        sandwich(self.emit(s), self.keep(GROUP), self.G, self.tab, self.times_h(-1.0))

    def detector(self, inten):
        def chi(p, zr, zi):
            meas = jnp.concatenate(
                [inten[i].reshape(W, W) for i in self.I[2 * p:2 * p + 2]], 1
            )
            ex = zr * zr + zi * zi - meas
            return zr * ex, zi * ex

        sandwich(self.phi(GROUP - 1), self.keep(GROUP), self.G, self.tab, chi)


def plan(place, mine, prev, offs, cols, srcs):
    d, t, last = place[0], place[1], place[2]
    for q in range(SLOTS):
        offs[q] = 0
        cols[q] = 0
        srcs[q] = 0
    n = jnp.int32(0)
    for q in range(SLOTS):
        stays = (q < mine[16]) & ((mine[q] <= RIM) | (t == last))
        comes = (q < prev[16]) & (prev[q] > RIM)
        take = jnp.where(d == 0, stays, comes)

        @pl.when(take)
        def _(q=q, n=n):
            offs[n] = jnp.where(d == 0, mine[q], prev[q] - RIM + INTS)
            cols[n] = jnp.where(d == 0, mine[8 + q], prev[8 + q])
            srcs[n] = q

        n = n + jnp.where(take, 1, 0)
    return n


class Core:
    def __init__(self, place, sem):
        self.d, self.sem = place[0], sem
        self.own_row = pl.multiple_of(jnp.where(self.d == 0, 0, RIM), 8)
        self.rim_row = pl.multiple_of(jnp.where(self.d == 0, W, 0), 8)

    def moves(self, s, own, rim, field, out):
        pairs = []
        for cb in range(BLOCKS):
            for k, (far, row, rows) in enumerate(
                ((own, self.own_row, W), (rim, self.rim_row, RIM))
            ):
                a = far.at[s, :, :, pl.ds(cb * W, W)]
                b = field.at[s, :, cb, pl.ds(row, rows), :]
                a, b = (b, a) if out else (a, b)
                pairs.append(pltpu.make_async_copy(a, b, self.sem.at[s, 2 * cb + k]))
        return pairs

    def fetch(self, owner, mine, other, rim, obj, downward=False):
        def one(i, _):
            s = GROUP - 1 - i if downward else i

            @pl.when(self.d == owner)
            def _():
                for c in self.moves(s, mine, rim, obj, False):
                    c.start()

            @pl.when(self.d != owner)
            def _():
                for c in self.moves(s, other, rim, obj, False):
                    c.start()

            return 0

        lax.fori_loop(0, GROUP, one, 0)

    def arrive(self, s, mine, rim, obj):
        for c in self.moves(s, mine, rim, obj, False):
            c.wait()

    def send(self, s, own, rim, acc):
        for c in self.moves(s, own, rim, acc, True):
            c.start()

    def gone(self, own, rim, acc):
        def one(s, _):
            for c in self.moves(s, own, rim, acc, True):
                c.wait()
            return 0

        lax.fori_loop(0, GROUP, one, 0)


def blank(obj):
    obj[:, :, :, W + RIM:, :] = jnp.zeros((GROUP, 2, BLOCKS, TALL - W - RIM, W), jnp.float32)


def clear(acc, s):
    acc[s] = jnp.zeros((2, BLOCKS, TALL, W), jnp.float32)


def sized(n, work):
    pl.when(n <= SIZES[0])(lambda: work(SIZES[0]))
    pl.when(n > SIZES[0])(lambda: work(SIZES[1]))


def first_kernel(
    place, mine, prev, my_own, other_own, rim, probe, H, tab, psi,
    obj, hist, offs, cols, srcs, sem, more,
):
    core = Core(place, sem)
    core.fetch(0, my_own, other_own, rim, obj)
    n = plan(place, mine, prev, offs, cols, srcs)
    blank(obj)

    def save(s):
        return pltpu.make_async_copy(hist.at[s + 1], psi.at[s], more.at[s])

    def work(G):
        step = Step(G, n, (offs, cols, srcs), obj, hist, H, tab)
        hist[0, :G * W, :] = jnp.concatenate([jnp.concatenate([probe[0], probe[1]], 1)] * G, 0)

        def ahead(s, _):
            core.arrive(s, my_own, rim, obj)
            step.forward(s)
            save(s).start()
            return 0

        lax.fori_loop(0, GROUP, ahead, 0)

    sized(n, work)
    for s in range(GROUP):
        save(s).wait()


def second_kernel(
    place, mine, prev, my_own, other_own, rim, low_rim, psi, ints, H, tab,
    out_own, out_rim, err,
    obj, acc, hist, inten, offs, cols, srcs, sem, more, isem,
):
    core = Core(place, sem)
    start = pltpu.make_async_copy(psi.at[GROUP - 1], hist.at[0], more.at[0])
    start.start()
    core.fetch(1, my_own, other_own, rim, obj)

    def near(q):
        return pltpu.make_async_copy(ints.at[q], inten.at[q], isem.at[q])

    def far(q, source):
        return [
            pltpu.make_async_copy(
                source.at[i, c, pl.ds(0, INTS), pl.ds((q % 4) * W, W)],
                inten.at[q, 2 * i + c],
                isem.at[8 + q * 8 + 2 * i + c],
            )
            for i in range(4) for c in range(2)
        ]

    def each(act):
        @pl.when(core.d == 0)
        def _():
            for q in range(SLOTS):
                act(near(q))

        @pl.when(core.d == 1)
        def _():
            for q in range(SLOTS):
                for c in far(q, low_rim if q < 4 else rim):
                    act(c)

    each(lambda c: c.start())
    n = plan(place, mine, prev, offs, cols, srcs)
    blank(obj)
    start.wait()

    def work(G):
        step = Step(G, n, (offs, cols, srcs), obj, hist, H, tab, acc)

        def ahead(s, _):
            core.arrive(s, my_own, rim, obj)
            step.forward(s)
            return 0

        lax.fori_loop(0, GROUP - 1, ahead, 0)
        core.arrive(GROUP - 1, my_own, rim, obj)
        each(lambda c: c.wait())
        step.detector(inten)

        def back(k, _):
            s = GROUP - 1 - k
            clear(acc, s)
            step.backward(s)
            core.send(s, out_own, out_rim, acc)
            return 0

        lax.fori_loop(0, GROUP, back, 0)

    sized(n, work)
    end = pltpu.make_async_copy(hist.at[GROUP], err, more.at[1])
    end.start()
    core.gone(out_own, out_rim, acc)
    end.wait()


def third_kernel(
    place, mine, prev, my_own, other_own, rim, psi, err, probe, H, tab,
    out_own, out_rim,
    obj, acc, hist, offs, cols, srcs, sem, more,
):
    core = Core(place, sem)

    def load(s):
        return pltpu.make_async_copy(psi.at[s - 1], hist.at[s], more.at[s])

    start = pltpu.make_async_copy(err, hist.at[GROUP], more.at[0])
    start.start()
    load(GROUP - 1).start()
    core.fetch(0, my_own, other_own, rim, obj, True)
    for s in range(GROUP - 2, 0, -1):
        load(s).start()
    n = plan(place, mine, prev, offs, cols, srcs)
    blank(obj)
    start.wait()

    def work(G):
        step = Step(G, n, (offs, cols, srcs), obj, hist, H, tab, acc)
        hist[0, :G * W, :] = jnp.concatenate([jnp.concatenate([probe[0], probe[1]], 1)] * G, 0)

        def back(k, _):
            s = GROUP - 1 - k
            clear(acc, s)
            load(s).wait()
            core.arrive(s, my_own, rim, obj)
            step.backward(s)
            core.send(s, out_own, out_rim, acc)
            return 0

        lax.fori_loop(0, GROUP - 1, back, 0)
        core.arrive(0, my_own, rim, obj)
        clear(acc, 0)
        for j in range(G):
            step.scatter(0, j)
        core.send(0, out_own, out_rim, acc)

    sized(n, work)
    core.gone(out_own, out_rim, acc)


def both_ways(value, outward):
    count = lax.axis_size("tile")
    up = [(i, i - 1) for i in range(1, count)]
    down = [(i, i + 1) for i in range(count - 1)]
    first, second = (down, up) if outward else (up, down)
    pairs = first + [(count + a, count + b) for a, b in second]
    return lax.ppermute(value, ("depth", "tile"), pairs)


def partner(value):
    return lax.ppermute(value, "depth", [(0, 1), (1, 0)])


def strips(value, by, source, target):
    count = lax.axis_size("tile")
    steps = [(i, i + by) for i in range(count) if 0 <= i + by < count]
    pairs = [(source * count + a, target * count + b) for a, b in steps]
    return lax.ppermute(value, ("depth", "tile"), pairs)


def packed(depth, above, below, ints):
    side = ints.reshape(4, 4, 2, INTS, W).transpose(1, 2, 3, 0, 4).reshape(4, 2, INTS, 4 * W)
    return jnp.where(
        depth == 0, above[:, :, :RIM], jnp.concatenate([side, below[:, :, RIM:]], axis=2)
    )


def local(
    specimen_layers,
    illumination_field,
    propagator_spectral_angle,
    recorded_intensities,
    patch_upper_edges,
    patch_left_edges,
    occupied_places_per_band,
):
    depth = lax.axis_index("depth")
    tile = lax.axis_index("tile")
    columns = specimen_layers.shape[3]
    count = lax.axis_size("tile")
    place = jnp.stack([depth, tile, jnp.int32(count - 1)]).astype(jnp.int32)
    mine = jnp.concatenate([patch_upper_edges, patch_left_edges, occupied_places_per_band])
    other = partner(specimen_layers)
    prev = strips(mine, 1, 1, 1)
    low = packed(depth, specimen_layers, other, recorded_intensities[:4])
    late_own, late_other, late_ints, low = lax.optimization_barrier(
        (specimen_layers, other, recorded_intensities[4:], low)
    )
    high = packed(depth, late_other, late_own, late_ints)
    low_rim = both_ways(low, False)
    high_rim = both_ways(high, False)
    H = jnp.stack([jnp.cos(propagator_spectral_angle), jnp.sin(propagator_spectral_angle)])
    tab = jnp.asarray(tables())
    hbm = pl.BlockSpec(memory_space=pl.ANY)
    vm = pl.BlockSpec(memory_space=pltpu.VMEM)
    sm = pl.BlockSpec(memory_space=pltpu.SMEM)
    own = jax.ShapeDtypeStruct((GROUP, 2, W, columns), jnp.float32)
    rim = jax.ShapeDtypeStruct((GROUP, 2, RIM, columns), jnp.float32)
    errors = jax.ShapeDtypeStruct((SLOTS * W, 2 * W), jnp.float32)
    field = pltpu.VMEM((GROUP, 2, BLOCKS, TALL, W), jnp.float32)
    hist = pltpu.VMEM((GROUP + 1, SLOTS * W, 2 * W), jnp.float32)
    tail = [pltpu.SMEM((SLOTS,), jnp.int32)] * 3 + [
        pltpu.SemaphoreType.DMA((GROUP, 2 * BLOCKS)),
        pltpu.SemaphoreType.DMA((GROUP,)),
    ]
    params = pltpu.CompilerParams(vmem_limit_bytes=48 * 1024 * 1024)
    where = (place, mine, prev, specimen_layers, other)
    psi = pl.pallas_call(
        first_kernel,
        out_shape=jax.ShapeDtypeStruct((GROUP, SLOTS * W, 2 * W), jnp.float32),
        in_specs=[sm] * 3 + [hbm] * 3 + [vm] * 3,
        out_specs=hbm,
        scratch_shapes=[field, hist] + tail,
        compiler_params=params,
        name="first",
    )(*where, low_rim, illumination_field, H, tab)
    own_high, rim_high, err = pl.pallas_call(
        second_kernel,
        out_shape=[own, rim, errors],
        in_specs=[sm] * 3 + [hbm] * 6 + [vm] * 2,
        out_specs=[hbm] * 3,
        scratch_shapes=[field, field, hist, pltpu.VMEM((SLOTS, 8, INTS, W), jnp.float32)]
        + tail + [pltpu.SemaphoreType.DMA((72,))],
        compiler_params=params,
        name="second",
    )(
        *where, high_rim, low_rim, psi,
        recorded_intensities.reshape(SLOTS, 8, INTS, W), H, tab,
    )
    came_high = both_ways(rim_high, True)
    own_low, rim_low = pl.pallas_call(
        third_kernel,
        out_shape=[own, rim],
        in_specs=[sm] * 3 + [hbm] * 5 + [vm] * 3,
        out_specs=[hbm] * 2,
        scratch_shapes=[field, field, hist] + tail,
        compiler_params=params,
        name="third",
    )(*where, low_rim, psi, err, illumination_field, H, tab)
    low_head = strips(rim_low, 1, 0, 0)
    low_foot = strips(rim_low, -1, 1, 0)
    head = jnp.concatenate([came_high, jnp.zeros((GROUP, 2, W - RIM, columns))], axis=2)
    given = jnp.where(depth == 0, own_high + head, own_low)
    taken = partner(given)
    foot = jnp.concatenate([jnp.zeros((GROUP, 2, RIM, columns)), came_high[:, :, INTS:]], axis=2)
    total = jnp.where(depth == 0, own_low, own_high + foot) + taken
    total = lax.optimization_barrier(total)
    return total + jnp.concatenate([low_head, low_foot[:, :, INTS:]], axis=2)


def solution(mesh):
    placed = (
        P("depth", None, "tile", None),
        P(),
        P(),
        P("tile", None, None),
        P("tile"),
        P("tile"),
        P("tile"),
    )
    return jax.shard_map(
        local, mesh=mesh, in_specs=placed, out_specs=P("depth", None, "tile", None), check_vma=False
    )
```
